128 devices in a mesh: row: 8 (over y, core), col: 16 (over z, x).
Axes of the slice: x: 4, y: 4, z: 4, core: 2. Of those that a mesh axis runs over, the one named last changes fastest.
Arguments:
- features: bfloat16 [262144, 256], P(('row', 'col')), may hold values from -6 to 6
- hub_features: bfloat16 [2048, 256], P(('row', 'col')), may hold values from -6 to 6
- w_self: bfloat16 [256, 256], replicated, may hold values from -0.375 to 0.375
- w_neigh: bfloat16 [256, 256], replicated, may hold values from -0.375 to 0.375
- out_bias: float32 [256], replicated, may hold values from -4 to 4
- local_edges: int32 [262144, 4], P(('row', 'col')), may hold values from 0 to 2047
- hub_edges: int32 [262144, 2], P(('row', 'col')), may hold values from 0 to 2047
- remote_edges: int32 [262144, 4], P(('row', 'col')), may hold values from 0 to 2047
- send_rows: int32 [128, 2048], P(('row', 'col')), may hold values from 0 to 2047
- cotangent: bfloat16 [262144, 256], P(('row', 'col')), may hold values from -6 to 6
Outputs:
- activated: bfloat16 [262144, 256], P(('row', 'col'))
- grad_features: float32 [262144, 256], P(('row', 'col'))
- grad_hubs: float32 [2048, 256], P(('row', 'col'))
- grad_w_self: float32 [256, 256], replicated
- grad_w_neigh: float32 [256, 256], replicated
- grad_bias: float32 [256], replicated
The draws below stay inside these ranges and needn't reach their ends.
All inputs are finite; a program needn't handle non-finite values.
Results may differ from the reference program's by a relative error of at most 0.0075.
Values may be sent and summed in bfloat16 or wider, within the bound.
A program may use at most 64 MiB of HBM per device.

```python
import math
import jax
import jax.numpy as jnp
import numpy as np

D = 256
NODE_DEV = 2048
BND = 16
FL = 4
FH = 2
FR = 4
NODES = 262144
HUBS = 2048
REMOTE = 2048
DEVICES = 128


def set_ends(array, rng, smallest, high):
    longest = array.shape.index(max(array.shape))
    spots = []
    for shift in (0, 1):
        where = [jax.random.randint(jax.random.fold_in(rng, axis), (), 0, length) for axis, length in enumerate(array.shape)]
        where[longest] = (where[longest] + shift) % array.shape[longest]
        spots.append(tuple(where))
    return array.at[spots[0]].set(smallest).at[spots[1]].set(high)


def steps_of(key, dims, pieces, least, top_value):
    factor_of, own = 1.0, jax.random.fold_in(key, 6)
    for dim, shards_of in pieces:
        heights = jnp.exp(jax.random.uniform(jax.random.fold_in(own, dim), (shards_of,), jnp.float32, least / len(pieces), top_value / len(pieces)))
        factor_of = factor_of * jnp.repeat(heights, dims[dim] // shards_of).reshape([-1 if axis == dim else 1 for axis in range(len(dims))])
    return factor_of


def rank_table(count, slope):
    weights = [(1 << 20) // math.isqrt(grade ** slope) + 1 for grade in range(1, count + 1)]
    spread = 1 + sum(weights) // (1 << 30)
    return np.cumsum(np.array([max(1, weight // spread) for weight in weights]))


def skewed_ids(rng, shape, amount, skew):
    table = rank_table(amount, skew)
    pick = jax.random.randint(jax.random.fold_in(rng, 1), shape, 0, int(table[amount - 1]))
    rank = jnp.searchsorted(jnp.asarray(table, jnp.int32), pick, side="right")
    return jax.random.permutation(jax.random.fold_in(rng, 2), amount)[rank].astype(jnp.int32)


def centred(key, dims, deviation, bound, shards=(), held_as=jnp.bfloat16):
    drawn = jax.random.normal(key, dims, jnp.float32) * deviation
    if len(shards) > 0:
        drawn = steps_of(key, dims, shards, -0.22, 0.18) * drawn
    return jnp.clip(drawn, min=-bound, max=bound).astype(held_as)


def setup_inputs(seed: int = 0) -> dict:
    keys = jax.random.split(jax.random.key(seed), 11)
    return {
        "features": centred(keys[0], (NODES, D), 1.0, 6.0, ((0, 128),)),
        "hub_features": centred(keys[1], (HUBS, D), 1.0, 6.0, ((0, 128),)),
        "w_self": centred(keys[2], (D, D), D ** -0.5, 0.375),
        "w_neigh": centred(keys[3], (D, D), D ** -0.5, 0.375),
        "out_bias": centred(keys[4], (D,), 1.0, 4.0, (), jnp.float32),
        "local_edges": set_ends(jax.random.randint(keys[5], (NODES, FL), 0, NODE_DEV), jax.random.fold_in(keys[5], 1), 0, NODE_DEV - 1).astype(jnp.int32),
        "hub_edges": set_ends(skewed_ids(keys[6], (NODES, FH), HUBS, 2), jax.random.fold_in(keys[6], 3), 0, HUBS - 1).astype(jnp.int32),
        "remote_edges": set_ends(jax.random.randint(keys[7], (NODES, FR), 0, REMOTE), jax.random.fold_in(keys[7], 1), 0, REMOTE - 1).astype(jnp.int32),
        "send_rows": set_ends(jax.random.randint(keys[8], (DEVICES, DEVICES * BND), 0, NODE_DEV), jax.random.fold_in(keys[8], 1), 0, NODE_DEV - 1).astype(jnp.int32),
        "cotangent": centred(keys[9], (NODES, D), 1.0, 6.0, ((0, 128),)),
    }


def reference(features, hub_features, w_self, w_neigh, out_bias, local_edges, hub_edges, remote_edges, send_rows, cotangent):
    node_count = features.shape[0]
    block = (jnp.arange(node_count, dtype=jnp.int32) // NODE_DEV)[:, None]
    local_index = (block * NODE_DEV + local_edges).astype(jnp.int32)
    source = remote_edges // BND
    slot = remote_edges % BND
    remote_rows = send_rows[source, block * BND + slot]
    remote_index = (source * NODE_DEV + remote_rows).astype(jnp.int32)
    fanout = FL + FH + FR
    summed = jnp.zeros(features.shape, jnp.float32)
    for column in range(FL):
        summed = summed + features[local_index[:, column]].astype(jnp.float32)
    for column in range(FH):
        summed = summed + hub_features[hub_edges[:, column]].astype(jnp.float32)
    for column in range(FR):
        summed = summed + features[remote_index[:, column]].astype(jnp.float32)
    neighbour_mean = (summed / fanout).astype(jnp.bfloat16)
    pre_act = jnp.dot(features, w_self, preferred_element_type=jnp.float32)
    pre_act = pre_act + jnp.dot(neighbour_mean, w_neigh, preferred_element_type=jnp.float32)
    pre_act = pre_act + out_bias.astype(jnp.float32)
    sigmoid_pre = jax.nn.sigmoid(pre_act)
    activated = (pre_act * sigmoid_pre).astype(jnp.bfloat16)
    grad_pre = (cotangent.astype(jnp.float32) * sigmoid_pre * (1.0 + pre_act * (1.0 - sigmoid_pre))).astype(jnp.bfloat16)
    grad_w_self = jnp.dot(features.T, grad_pre, preferred_element_type=jnp.float32)
    grad_w_neigh = jnp.dot(neighbour_mean.T, grad_pre, preferred_element_type=jnp.float32)
    grad_bias = jnp.sum(grad_pre.astype(jnp.float32), axis=0)
    grad_mean = jnp.dot(grad_pre, w_neigh.T, preferred_element_type=jnp.float32) / fanout
    grad_features = jnp.dot(grad_pre, w_self.T, preferred_element_type=jnp.float32)
    for column in range(FL):
        grad_features = grad_features.at[local_index[:, column]].add(grad_mean)
    for column in range(FR):
        grad_features = grad_features.at[remote_index[:, column]].add(grad_mean)
    grad_hubs = jnp.zeros(hub_features.shape, jnp.float32)
    for column in range(FH):
        grad_hubs = grad_hubs.at[hub_edges[:, column]].add(grad_mean)
    return (activated, grad_features, grad_hubs, grad_w_self, grad_w_neigh, grad_bias)
```

```python
import functools

import jax
import jax.numpy as jnp
from jax import lax
from jax.experimental import pallas as pl
from jax.experimental.pallas import tpu as pltpu
from jax.sharding import PartitionSpec as P

MESH = pl.DeviceIdType.MESH
F32 = jnp.float32
BF16 = jnp.bfloat16
TILE = 256


def kernel(
    rows_n,
    cols_n,
    fanouts,
    x_ref,
    hub_ref,
    ws_ref,
    wn_ref,
    bias_ref,
    el_ref,
    eh_ref,
    er_ref,
    es_ref,
    cot_ref,
    act_ref,
    gf_ref,
    ghub_ref,
    gws_ref,
    gwn_ref,
    gb_ref,
    erow,
    ecol,
    c_hub,
    c_rem,
    t_hub,
    t_rem,
    blk,
    send1,
    recv1,
    hub_all,
    send2,
    recv2,
    gm,
    pair_out,
    pair_in,
    hub_own,
    hub_send,
    hub_recv,
    wpart,
    wpair,
    wfinal,
    wrecv,
    wown,
    wtot,
    bpart,
    bpair,
    brecv,
    s_send,
    s_hub,
    s_hubp,
    s_bnd,
    s_wpair,
    s_w,
    s_b,
    s_gb,
    s_gpair,
    s_ghub,
    s_wag,
    s_wagp,
):
    fl, fh, fr = fanouts
    fanout = fl + fh + fr
    nodes, width = x_ref.shape
    tiles = nodes // TILE
    bnd = send1.shape[1]
    row = lax.axis_index("row")
    col = lax.axis_index("col")
    core = lax.rem(row, 2)
    yy = row // 2
    me = row * cols_n + col
    partner = (row + 1 - 2 * core, col)
    chips = rows_n // 2 * cols_n
    total = rows_n * cols_n
    chip = yy * cols_n + col

    def each_chip(fn):
        def outer(i, c):
            def inner(j, cc):
                y2 = lax.rem(yy + i, rows_n // 2)
                c2 = lax.rem(col + j, cols_n)

                @pl.when((i + j) > 0)
                def _():
                    fn(y2, c2)

                return cc

            return lax.fori_loop(0, cols_n, inner, c)

        lax.fori_loop(0, rows_n // 2, outer, 0)

    def remote(src, dst, ssem, rsem, dev):
        return pltpu.make_async_remote_copy(
            src_ref=src, dst_ref=dst, send_sem=ssem, recv_sem=rsem, device_id=dev, device_id_type=MESH
        )

    def drain(ref, sem):
        pltpu.make_async_copy(ref, ref, sem).wait()

    barrier = pltpu.get_barrier_semaphore()

    def greet_row(i, c):
        def greet(j, cc):
            @pl.when((i + j) > 0)
            def _():
                pl.semaphore_signal(
                    barrier,
                    inc=1,
                    device_id=(lax.rem(row + i, rows_n), lax.rem(col + j, cols_n)),
                    device_id_type=MESH,
                )

            return cc

        return lax.fori_loop(0, cols_n, greet, c)

    lax.fori_loop(0, rows_n, greet_row, 0)

    erow[...] = jnp.concatenate(
        [
            el_ref[...].astype(F32),
            eh_ref[...].astype(F32),
            er_ref[...].astype(F32),
            es_ref[...].astype(F32),
            jnp.zeros((16 - fanout - 1, nodes), F32),
        ],
        axis=0,
    )
    ecol[...] = erow[...].T
    local = range(0, fl)
    hubs = range(fl, fl + fh)
    remotes = range(fl + fh, fanout)
    lists = range(fanout, fanout + 1)

    lane_id = lax.broadcasted_iota(jnp.int32, (TILE, TILE), 1).astype(F32).astype(BF16)
    sub_id = lax.broadcasted_iota(jnp.int32, (TILE, TILE), 0).astype(F32).astype(BF16)
    one = jnp.ones((TILE, TILE), BF16)
    zero = jnp.zeros((TILE, TILE), BF16)

    def build_col(dst, dst_row, nb, js):
        edges = ecol[pl.ds(nb * TILE, TILE), :]
        for t in range(tiles):
            shifted = (edges - float(TILE * t)).astype(BF16)
            acc = None
            for j in js:
                hit = jnp.where(shifted[:, j : j + 1] == lane_id, one, zero)
                acc = hit if acc is None else acc + hit
            dst[pl.ds(dst_row, TILE), pl.ds(t * TILE, TILE)] = acc

    def build_row(dst, dst_row, rb, js):
        base = (rb * TILE).astype(F32)
        for t in range(tiles):
            shifted = (erow[:, pl.ds(t * TILE, TILE)] - base).astype(BF16)
            acc = None
            for j in js:
                hit = jnp.where(shifted[j : j + 1, :] == sub_id, one, zero)
                acc = hit if acc is None else acc + hit
            dst[pl.ds(dst_row, TILE), pl.ds(t * TILE, TILE)] = acc

    def dot(a, b):
        return jnp.dot(a, b, preferred_element_type=F32)

    pl.semaphore_wait(barrier, total - 1)

    hub_all[pl.ds(me * bnd, bnd), :] = hub_ref[...]
    each_chip(
        lambda y2, c2: remote(
            hub_ref, hub_all.at[pl.ds(me * bnd, bnd)], s_send.at[0], s_hub, (y2 * 2 + core, c2)
        ).start()
    )

    def send_row(i, c, src, dst, ssem, rsem):
        r2 = lax.rem(row + i, rows_n)

        def one_dest(j, cc):
            c2 = lax.rem(col + j, cols_n)

            @pl.when((i + j) > 0)
            def _():
                remote(src.at[r2 * cols_n + c2], dst.at[me], ssem, rsem, (r2, c2)).start()

            return cc

        return lax.fori_loop(0, cols_n, one_dest, c)

    def pick(i, c):
        r2 = lax.rem(row + i, rows_n)
        build_col(blk, 0, r2, lists)
        picked = dot(blk[...], x_ref[...]).astype(BF16)
        send1[pl.ds(r2 * cols_n, cols_n)] = picked.reshape(cols_n, bnd, width)
        return send_row(i, c, send1, recv1, s_send.at[1], s_bnd)

    lax.fori_loop(0, rows_n, pick, 0)
    recv1[me] = send1[me]

    def local_part(nb, c):
        build_col(blk, 0, nb, local)
        gf_ref[pl.ds(nb * TILE, TILE), :] = dot(blk[...], x_ref[...])
        build_col(c_hub, nb * TILE, nb, hubs)
        return c

    lax.fori_loop(0, tiles, local_part, 0)

    drain(hub_all.at[pl.ds(0, (chips - 1) * bnd)], s_hub)
    for y2 in range(rows_n // 2):
        part = hub_all.at[pl.ds((y2 * 2 + core) * TILE, TILE)]
        remote(part, part, s_send.at[2], s_hubp, partner).start()

    def counts_part(nb, c):
        build_col(c_rem, nb * TILE, nb, remotes)
        build_row(t_rem, nb * TILE, nb, remotes)
        build_row(t_hub, nb * TILE, nb, hubs)
        return c

    lax.fori_loop(0, tiles, counts_part, 0)
    drain(hub_all.at[pl.ds(0, rows_n // 2 * TILE)], s_hubp)

    def hub_part(nb, c):
        rows = pl.ds(nb * TILE, TILE)
        gf_ref[rows, :] += dot(c_hub[rows, :], hub_all[...])
        return c

    lax.fori_loop(0, tiles, hub_part, 0)
    drain(recv1.at[pl.ds(0, total - 1)], s_bnd)

    wpart[...] = jnp.zeros_like(wpart)
    bpart[...] = jnp.zeros_like(bpart)
    ta = (((0,), (0,)), ((), ()))
    tb = (((1,), (1,)), ((), ()))

    def dense(nb, c):
        rows = pl.ds(nb * TILE, TILE)
        incoming = recv1[...].reshape(total * bnd, width)
        summed = gf_ref[rows, :] + dot(c_rem[rows, :], incoming)
        mean = (summed / float(fanout)).astype(BF16)
        x = x_ref[rows, :]
        pre = dot(x, ws_ref[...]) + dot(mean, wn_ref[...]) + bias_ref[...]
        sig = jax.nn.sigmoid(pre)
        act_ref[rows, :] = (pre * sig).astype(BF16)
        gp = (cot_ref[rows, :].astype(F32) * sig * (1.0 + pre * (1.0 - sig))).astype(BF16)
        wpart[0] += lax.dot_general(x, gp, ta, preferred_element_type=F32)
        wpart[1] += lax.dot_general(mean, gp, ta, preferred_element_type=F32)
        bpart[0:1, :] += jnp.sum(gp.astype(F32), axis=0, keepdims=True)
        gm[rows, :] = (
            lax.dot_general(gp, wn_ref[...], tb, preferred_element_type=F32) / float(fanout)
        ).astype(BF16)
        gf_ref[rows, :] = lax.dot_general(gp, ws_ref[...], tb, preferred_element_type=F32)
        return c

    lax.fori_loop(0, tiles, dense, 0)

    remote(wpart.at[1 - core], wpair, s_send.at[3], s_wpair.at[0], partner).start()
    remote(bpart, bpair, s_send.at[4], s_wpair.at[1], partner).start()

    def spread_block(i, c):
        r2 = lax.rem(row + i, rows_n)
        out = dot(t_rem[pl.ds(r2 * TILE, TILE), :], gm[...]).astype(BF16)
        send2[pl.ds(r2 * cols_n, cols_n)] = out.reshape(cols_n, bnd, width)
        return send_row(i, c, send2, recv2, s_send.at[5], s_gb)

    spread_block(0, 0)
    drain(wpair, s_wpair.at[0])
    drain(bpair, s_wpair.at[1])
    wfinal[...] = wpart[core] + wpair[...]
    brecv[chip] = bpart[0:1, :] + bpair[0:1, :]

    def send_weights(y2, c2):
        other = y2 * cols_n + c2
        remote(
            wfinal.at[pl.ds(other // 2 * 8, 8), pl.ds(lax.rem(other, 2) * 128, 128)],
            wrecv.at[chip],
            s_send.at[6],
            s_w,
            (y2 * 2 + core, c2),
        ).start()
        remote(brecv.at[chip], brecv.at[chip], s_send.at[7], s_b, (y2 * 2 + core, c2)).start()

    each_chip(send_weights)
    wrecv[chip] = wfinal[pl.ds(chip // 2 * 8, 8), pl.ds(pl.multiple_of(lax.rem(chip, 2) * 128, 128), 128)]
    lax.fori_loop(1, rows_n, spread_block, 0)
    recv2[me] = send2[me]

    def hub_other(y2, c):
        r2 = y2 * 2 + 1 - core
        pair_out[pl.ds(y2 * TILE, TILE), :] = dot(
            t_hub[pl.ds(r2 * TILE, TILE), :], gm[...]
        ).astype(BF16)
        return c

    lax.fori_loop(0, rows_n // 2, hub_other, 0)
    remote(pair_out, pair_in, s_send.at[8], s_gpair, partner).start()

    def hub_mine(y2, c):
        r2 = y2 * 2 + core
        hub_own[pl.ds(y2 * TILE, TILE), :] = dot(t_hub[pl.ds(r2 * TILE, TILE), :], gm[...])
        return c

    lax.fori_loop(0, rows_n // 2, hub_mine, 0)
    drain(pair_in, s_gpair)

    def hub_join(y2, c):
        rows = pl.ds(y2 * TILE, TILE)
        both = (hub_own[rows, :] + pair_in[rows, :].astype(F32)).astype(BF16)
        hub_send[pl.ds(y2 * cols_n, cols_n)] = both.reshape(cols_n, bnd, width)
        return c

    lax.fori_loop(0, rows_n // 2, hub_join, 0)
    each_chip(
        lambda y2, c2: remote(
            hub_send.at[y2 * cols_n + c2],
            hub_recv.at[chip],
            s_send.at[9],
            s_ghub,
            (y2 * 2 + core, c2),
        ).start()
    )
    hub_recv[chip] = hub_send[chip]

    drain(wrecv.at[pl.ds(0, chips - 1)], s_w)
    drain(brecv.at[pl.ds(0, chips - 1)], s_b)
    own_tile = (pl.ds(pl.multiple_of(chip // 2 * 8, 8), 8), pl.ds(pl.multiple_of(lax.rem(chip, 2) * 128, 128), 128))
    wown[...] = jnp.sum(wrecv[...], axis=0)
    each_chip(
        lambda y2, c2: remote(
            wown, wtot.at[core].at[own_tile], s_send.at[10], s_wag, (y2 * 2 + core, c2)
        ).start()
    )
    wtot[(core,) + own_tile] = wown[...]
    gb_ref[...] = jnp.sum(brecv[...], axis=0)

    def local_back(rb, c):
        build_row(blk, 0, rb, local)
        gf_ref[pl.ds(rb * TILE, TILE), :] += dot(blk[...], gm[...])
        return c

    lax.fori_loop(0, tiles, local_back, 0)
    drain(wrecv.at[pl.ds(0, chips - 1)], s_wag)
    remote(wtot.at[core], wtot.at[core], s_send.at[11], s_wagp, partner).start()

    def return_counts(rb, c):
        build_row(c_rem, rb * TILE, rb, lists)
        return c

    lax.fori_loop(0, tiles, return_counts, 0)
    drain(wtot.at[0], s_wagp)
    gws_ref[...] = wtot[0]
    gwn_ref[...] = wtot[1]
    drain(recv2.at[pl.ds(0, total - 1)], s_gb)

    def return_block(rb, c):
        rows = pl.ds(rb * TILE, TILE)
        gf_ref[rows, :] += dot(c_rem[rows, :], recv2[...].reshape(total * bnd, width))
        return c

    lax.fori_loop(0, tiles, return_block, 0)
    drain(hub_recv.at[pl.ds(0, chips - 1)], s_ghub)
    ghub_ref[...] = jnp.sum(hub_recv[...].astype(F32), axis=0)

    drain(hub_all.at[pl.ds(0, (chips - 1) * bnd)], s_send.at[0])
    drain(recv1.at[pl.ds(0, total - 1)], s_send.at[1])
    drain(pair_in, s_send.at[2])
    drain(wpair, s_send.at[3])
    drain(bpair, s_send.at[4])
    drain(recv1.at[pl.ds(0, total - 1)], s_send.at[5])
    drain(wrecv.at[pl.ds(0, chips - 1)], s_send.at[6])
    drain(brecv.at[pl.ds(0, chips - 1)], s_send.at[7])
    drain(pair_in, s_send.at[8])
    drain(hub_recv.at[pl.ds(0, chips - 1)], s_send.at[9])
    drain(wrecv.at[pl.ds(0, chips - 1)], s_send.at[10])
    drain(wpair, s_send.at[11])


def solution(mesh):
    rows_n, cols_n = mesh.shape["row"], mesh.shape["col"]

    def body(
        features,
        hub_features,
        w_self,
        w_neigh,
        out_bias,
        local_edges,
        hub_edges,
        remote_edges,
        send_rows,
        cotangent,
    ):
        nodes, width = features.shape
        hub_own = hub_features.shape[0]
        total = rows_n * cols_n
        chips = total // 2
        bnd = send_rows.shape[1] // total
        hubs = hub_own * total
        fanouts = (local_edges.shape[1], hub_edges.shape[1], remote_edges.shape[1])
        vmem = pl.BlockSpec(memory_space=pltpu.VMEM)
        dma = pltpu.SemaphoreType.DMA
        outs = pl.pallas_call(
            functools.partial(kernel, rows_n, cols_n, fanouts),
            out_shape=(
                jax.ShapeDtypeStruct((nodes, width), BF16),
                jax.ShapeDtypeStruct((nodes, width), F32),
                jax.ShapeDtypeStruct((hub_own, width), F32),
                jax.ShapeDtypeStruct((width, width), F32),
                jax.ShapeDtypeStruct((width, width), F32),
                jax.ShapeDtypeStruct((1, width), F32),
            ),
            in_specs=[vmem] * 10,
            out_specs=(vmem,) * 6,
            scratch_shapes=[
                pltpu.VMEM((16, nodes), F32),
                pltpu.VMEM((nodes, 16), F32),
                pltpu.VMEM((nodes, hubs), BF16),
                pltpu.VMEM((nodes, total * bnd), BF16),
                pltpu.VMEM((hubs, nodes), BF16),
                pltpu.VMEM((total * bnd, nodes), BF16),
                pltpu.VMEM((TILE, nodes), BF16),
                pltpu.VMEM((total, bnd, width), BF16),
                pltpu.VMEM((total, bnd, width), BF16),
                pltpu.VMEM((hubs, width), BF16),
                pltpu.VMEM((total, bnd, width), BF16),
                pltpu.VMEM((total, bnd, width), BF16),
                pltpu.VMEM((nodes, width), BF16),
                pltpu.VMEM((hubs // 2, width), BF16),
                pltpu.VMEM((hubs // 2, width), BF16),
                pltpu.VMEM((hubs // 2, width), F32),
                pltpu.VMEM((chips, hub_own, width), BF16),
                pltpu.VMEM((chips, hub_own, width), BF16),
                pltpu.VMEM((2, width, width), F32),
                pltpu.VMEM((width, width), F32),
                pltpu.VMEM((width, width), F32),
                pltpu.VMEM((chips, 8, 128), F32),
                pltpu.VMEM((8, 128), F32),
                pltpu.VMEM((2, width, width), F32),
                pltpu.VMEM((8, width), F32),
                pltpu.VMEM((8, width), F32),
                pltpu.VMEM((chips, 1, width), F32),
                dma((12,)),
                dma,
                dma,
                dma,
                dma((2,)),
                dma,
                dma,
                dma,
                dma,
                dma,
                dma,
                dma,
            ],
            compiler_params=pltpu.CompilerParams(
                collective_id=0, has_side_effects=True, vmem_limit_bytes=60 << 20
            ),
        )(
            features,
            hub_features,
            w_self,
            w_neigh,
            out_bias.reshape(1, width),
            local_edges.T,
            hub_edges.T,
            remote_edges.T,
            send_rows,
            cotangent,
        )
        activated, grad_features, grad_hubs, grad_w_self, grad_w_neigh, grad_bias = outs
        return activated, grad_features, grad_hubs, grad_w_self, grad_w_neigh, grad_bias.reshape(width)

    by_node = P(("row", "col"), None)
    return jax.shard_map(
        body,
        mesh=mesh,
        in_specs=(by_node, by_node, P(), P(), P(), by_node, by_node, by_node, by_node, by_node),
        out_specs=(by_node, by_node, by_node, P(), P(), P()),
        check_vma=False,
    )
```

```python
import functools

import jax
import jax.numpy as jnp
from jax import lax
from jax.experimental import pallas as pl
from jax.experimental.pallas import tpu as pltpu
from jax.sharding import PartitionSpec as P

MESH = pl.DeviceIdType.MESH
F32 = jnp.float32
BF16 = jnp.bfloat16
TILE = 256
BIG = 512


def kernel(
    rows_n,
    cols_n,
    fanouts,
    x_in,
    hub_ref,
    ws_ref,
    wn_ref,
    bias_ref,
    el_ref,
    eh_ref,
    er_ref,
    es_ref,
    cot_in,
    act_out,
    gf_out,
    ghub_ref,
    gws_ref,
    gwn_ref,
    gb_ref,
    x_ref,
    cot_ref,
    act_ref,
    gf_ref,
    mean_ref,
    gp_ref,
    erow,
    ecol,
    c_hub,
    c_rem,
    t_rem,
    blk,
    send1,
    recv1,
    hub_all,
    send2,
    recv2,
    gm,
    pair_out,
    pair_in,
    hub_own,
    hub_send,
    hub_recv,
    wpart,
    wpair,
    wsend,
    wrecv,
    wown,
    wtot,
    bpart,
    bpair,
    brecv,
    s_send,
    s_hub,
    s_hubp,
    s_bnd,
    s_wpair,
    s_w,
    s_b,
    s_gb,
    s_gpair,
    s_ghub,
    s_wag,
    s_wagp,
    s_io,
):
    fl, fh, fr = fanouts
    fanout = fl + fh + fr
    nodes, width = x_ref.shape
    x_copy = pltpu.make_async_copy(x_in, x_ref, s_io.at[0])
    x_copy.start()
    cot_copy = pltpu.make_async_copy(cot_in, cot_ref, s_io.at[1])
    cot_copy.start()
    tiles = nodes // TILE
    bnd = send1.shape[1]
    row = lax.axis_index("row")
    col = lax.axis_index("col")
    core = lax.rem(row, 2)
    yy = row // 2
    me = row * cols_n + col
    partner = (row + 1 - 2 * core, col)
    chips = rows_n // 2 * cols_n
    total = rows_n * cols_n
    chip = yy * cols_n + col

    def far(i):
        return lax.rem(2 + 3 * i + 3 * (i // 2) + 2 * (i // 3), 4)

    def far_col(j):
        z2 = lax.rem(col // 4 + far(j // 4), 4)
        return z2 * 4 + lax.rem(col + far(lax.rem(j, 4)), 4)

    def far_row(i):
        return lax.rem(yy + far(i // 2), 4) * 2 + lax.rem(core + 1 + i, 2)

    def each_chip(fn):
        def one_chip(k, c):
            fn(lax.rem(yy + far(k // cols_n), 4), far_col(lax.rem(k, cols_n)))
            return c

        lax.fori_loop(0, chips - 1, one_chip, 0)

    def remote(src, dst, ssem, rsem, dev):
        return pltpu.make_async_remote_copy(
            src_ref=src, dst_ref=dst, send_sem=ssem, recv_sem=rsem, device_id=dev, device_id_type=MESH
        )

    def drain(ref, sem):
        pltpu.make_async_copy(ref, ref, sem).wait()

    barrier = pltpu.get_barrier_semaphore()

    def greet(k, c):
        pl.semaphore_signal(
            barrier,
            inc=1,
            device_id=(far_row(k // cols_n), far_col(lax.rem(k, cols_n))),
            device_id_type=MESH,
        )
        return c

    lax.fori_loop(0, total - 1, greet, 0)

    erow[...] = jnp.concatenate(
        [
            el_ref[...].astype(F32),
            eh_ref[...].astype(F32),
            er_ref[...].astype(F32),
            es_ref[...].astype(F32),
            jnp.zeros((16 - fanout - 1, nodes), F32),
        ],
        axis=0,
    )
    ecol[...] = erow[...].T
    local = range(0, fl)
    hubs = range(fl, fl + fh)
    remotes = range(fl + fh, fanout)
    lists = range(fanout, fanout + 1)

    lane_id = lax.broadcasted_iota(jnp.int32, (TILE, TILE), 1).astype(F32).astype(BF16)
    sub_id = lax.broadcasted_iota(jnp.int32, (TILE, TILE), 0).astype(F32).astype(BF16)
    one = jnp.ones((TILE, TILE), BF16)
    zero = jnp.zeros((TILE, TILE), BF16)

    def build_col(dst, dst_row, nb, js):
        edges = ecol[pl.ds(nb * TILE, TILE), :]
        for t in range(tiles):
            shifted = (edges - float(TILE * t)).astype(BF16)
            acc = None
            for j in js:
                hit = jnp.where(shifted[:, j : j + 1] == lane_id, one, zero)
                acc = hit if acc is None else acc + hit
            dst[pl.ds(dst_row, TILE), pl.ds(t * TILE, TILE)] = acc

    def build_row(dst, dst_row, rb, js):
        base = (rb * TILE).astype(F32)
        for t in range(tiles):
            shifted = (erow[:, pl.ds(t * TILE, TILE)] - base).astype(BF16)
            acc = None
            for j in js:
                hit = jnp.where(shifted[j : j + 1, :] == sub_id, one, zero)
                acc = hit if acc is None else acc + hit
            dst[pl.ds(dst_row, TILE), pl.ds(t * TILE, TILE)] = acc

    def dot(a, b):
        return jnp.dot(a, b, preferred_element_type=F32)

    pl.semaphore_wait(barrier, total - 1)

    hub_all[pl.ds(me * bnd, bnd), :] = hub_ref[...]
    each_chip(
        lambda y2, c2: remote(
            hub_ref, hub_all.at[pl.ds(me * bnd, bnd)], s_send.at[0], s_hub, (y2 * 2 + core, c2)
        ).start()
    )

    def send_row(i, count, src, dst, ssem, rsem):
        r2 = far_row(i)

        def one_dest(j, c):
            c2 = far_col(j)
            remote(src.at[r2 * cols_n + c2], dst.at[me], ssem, rsem, (r2, c2)).start()
            return c

        lax.fori_loop(0, count, one_dest, 0)

    def pick(i):
        r2 = far_row(i)
        build_col(blk, 0, r2, lists)
        picked = dot(blk[pl.ds(0, TILE), :], x_ref[...]).astype(BF16)
        send1[pl.ds(r2 * cols_n, cols_n)] = picked.reshape(cols_n, bnd, width)

    def pick_and_send(i, c):
        pick(i)
        send_row(i, cols_n, send1, recv1, s_send.at[1], s_bnd)
        return c

    x_copy.wait()
    lax.fori_loop(0, rows_n - 1, pick_and_send, 0)
    pick(rows_n - 1)
    send_row(rows_n - 1, cols_n - 1, send1, recv1, s_send.at[1], s_bnd)
    recv1[me] = send1[me]

    def local_part(nb, c):
        build_col(blk, 0, nb, local)
        gf_ref[pl.ds(nb * TILE, TILE), :] = dot(blk[pl.ds(0, TILE), :], x_ref[...])
        build_col(c_hub, nb * TILE, nb, hubs)
        return c

    lax.fori_loop(0, tiles, local_part, 0)

    drain(hub_all.at[pl.ds(0, (chips - 1) * bnd)], s_hub)
    for y2 in range(rows_n // 2):
        part = hub_all.at[pl.ds((y2 * 2 + core) * TILE, TILE)]
        remote(part, part, s_send.at[2], s_hubp, partner).start()

    def counts_part(nb, c):
        build_col(c_rem, nb * TILE, nb, remotes)
        build_row(t_rem, nb * TILE, nb, remotes)
        return c

    lax.fori_loop(0, tiles, counts_part, 0)
    drain(hub_all.at[pl.ds(0, rows_n // 2 * TILE)], s_hubp)

    def hub_part(nb, c):
        rows = pl.ds(nb * BIG, BIG)
        gf_ref[rows, :] += dot(c_hub[rows, :], hub_all[...])
        return c

    lax.fori_loop(0, nodes // BIG, hub_part, 0)
    drain(recv1.at[pl.ds(0, total - 1)], s_bnd)

    ta = (((0,), (0,)), ((), ()))
    tb = (((1,), (1,)), ((), ()))
    cot_copy.wait()

    def dense(nb, c):
        rows = pl.ds(nb * BIG, BIG)
        incoming = recv1[...].reshape(total * bnd, width)
        summed = gf_ref[rows, :] + dot(c_rem[rows, :], incoming)
        mean = (summed / float(fanout)).astype(BF16)
        mean_ref[rows, :] = mean
        pre = dot(x_ref[rows, :], ws_ref[...]) + dot(mean, wn_ref[...]) + bias_ref[...]
        sig = jax.nn.sigmoid(pre)
        act_ref[rows, :] = (pre * sig).astype(BF16)
        gp_ref[rows, :] = (
            cot_ref[rows, :].astype(F32) * sig * (1.0 + pre * (1.0 - sig))
        ).astype(BF16)
        return c

    lax.fori_loop(0, nodes // BIG, dense, 0)
    act_copy = pltpu.make_async_copy(act_ref, act_out, s_io.at[2])
    act_copy.start()

    def back_mean(nb, c):
        rows = pl.ds(nb * BIG, BIG)
        gm[rows, :] = (
            lax.dot_general(gp_ref[rows, :], wn_ref[...], tb, preferred_element_type=F32) / float(fanout)
        ).astype(BF16)
        return c

    lax.fori_loop(0, nodes // BIG, back_mean, 0)
    wpart[0] = lax.dot_general(x_ref[...], gp_ref[...], ta, preferred_element_type=F32)
    wpart[1] = lax.dot_general(mean_ref[...], gp_ref[...], ta, preferred_element_type=F32)
    bpart[0:1, :] = jnp.sum(gp_ref[...].astype(F32), axis=0, keepdims=True)
    remote(wpart.at[1 - core], wpair, s_send.at[3], s_wpair.at[0], partner).start()
    remote(bpart, bpair, s_send.at[4], s_wpair.at[1], partner).start()

    def spread_block(i):
        r2 = far_row(i)
        out = dot(t_rem[pl.ds(r2 * TILE, TILE), :], gm[...]).astype(BF16)
        send2[pl.ds(r2 * cols_n, cols_n)] = out.reshape(cols_n, bnd, width)

    def spread_and_send(i, c):
        spread_block(i)
        send_row(i, cols_n, send2, recv2, s_send.at[5], s_gb)
        return c

    spread_and_send(jnp.int32(0), 0)
    drain(wpair, s_wpair.at[0])
    drain(bpair, s_wpair.at[1])
    both = wpart[core] + wpair[...]
    for h in range(2):
        wsend[pl.ds(h * (chips // 2), chips // 2)] = both[:, h * 128 : h * 128 + 128].astype(BF16).reshape(chips // 2, 8, 128)
    brecv[chip] = bpart[0:1, :] + bpair[0:1, :]

    def send_weights(y2, c2):
        dev = (y2 * 2 + core, c2)
        remote(wsend.at[y2 * cols_n + c2], wrecv.at[chip], s_send.at[6], s_w, dev).start()
        remote(brecv.at[chip], brecv.at[chip], s_send.at[7], s_b, dev).start()

    each_chip(send_weights)
    wrecv[chip] = wsend[chip]
    lax.fori_loop(1, rows_n - 1, spread_and_send, 0)
    spread_block(rows_n - 1)
    send_row(rows_n - 1, cols_n - 1, send2, recv2, s_send.at[5], s_gb)
    recv2[me] = send2[me]

    def hub_other(y2, c):
        r2 = y2 * 2 + 1 - core
        build_row(blk, 0, r2, hubs)
        pair_out[pl.ds(y2 * TILE, TILE), :] = dot(
            blk[pl.ds(0, TILE), :], gm[...]
        ).astype(BF16)
        return c

    lax.fori_loop(0, rows_n // 2, hub_other, 0)
    remote(pair_out, pair_in, s_send.at[8], s_gpair, partner).start()

    def hub_mine(y2, c):
        r2 = y2 * 2 + core
        build_row(blk, 0, r2, hubs)
        hub_own[pl.ds(y2 * TILE, TILE), :] = dot(blk[pl.ds(0, TILE), :], gm[...])
        return c

    lax.fori_loop(0, rows_n // 2, hub_mine, 0)
    drain(pair_in, s_gpair)

    def hub_join(y2, c):
        rows = pl.ds(y2 * TILE, TILE)
        both = (hub_own[rows, :] + pair_in[rows, :].astype(F32)).astype(BF16)
        hub_send[pl.ds(y2 * cols_n, cols_n)] = both.reshape(cols_n, bnd, width)
        return c

    lax.fori_loop(0, rows_n // 2, hub_join, 0)
    each_chip(
        lambda y2, c2: remote(
            hub_send.at[y2 * cols_n + c2],
            hub_recv.at[chip],
            s_send.at[9],
            s_ghub,
            (y2 * 2 + core, c2),
        ).start()
    )
    hub_recv[chip] = hub_send[chip]

    drain(wrecv.at[pl.ds(0, chips - 1)], s_w)
    drain(brecv.at[pl.ds(0, chips - 1)], s_b)
    wown[...] = jnp.sum(wrecv[...].astype(F32), axis=0).astype(BF16)
    each_chip(
        lambda y2, c2: remote(
            wown, wtot.at[core, chip], s_send.at[10], s_wag, (y2 * 2 + core, c2)
        ).start()
    )
    wtot[core, chip] = wown[...]
    gb_ref[...] = jnp.sum(brecv[...], axis=0)

    def local_back(rb, c):
        rows = pl.ds(rb * TILE, TILE)
        build_row(blk, 0, rb, local)
        gf_ref[rows, :] = dot(blk[pl.ds(0, TILE), :], gm[...]) + lax.dot_general(
            gp_ref[rows, :], ws_ref[...], tb, preferred_element_type=F32
        )
        return c

    lax.fori_loop(0, tiles, local_back, 0)
    drain(wrecv.at[pl.ds(0, chips - 1)], s_wag)
    remote(wtot.at[core], wtot.at[core], s_send.at[11], s_wagp, partner).start()

    def return_counts(rb, c):
        build_row(c_rem, rb * TILE, rb, lists)
        return c

    lax.fori_loop(0, tiles, return_counts, 0)
    drain(wtot.at[0], s_wagp)
    for h in range(2):
        part = pl.ds(h * (chips // 2), chips // 2)
        gws_ref[:, pl.ds(h * 128, 128)] = wtot[0, part].astype(F32).reshape(width, 128)
        gwn_ref[:, pl.ds(h * 128, 128)] = wtot[1, part].astype(F32).reshape(width, 128)
    drain(recv2.at[pl.ds(0, total - 1)], s_gb)

    def return_block(rb, c):
        rows = pl.ds(rb * BIG, BIG)
        gf_ref[rows, :] += dot(c_rem[rows, :], recv2[...].reshape(total * bnd, width))
        return c

    lax.fori_loop(0, nodes // BIG, return_block, 0)
    gf_copy = pltpu.make_async_copy(gf_ref, gf_out, s_io.at[3])
    gf_copy.start()
    drain(hub_recv.at[pl.ds(0, chips - 1)], s_ghub)
    ghub_ref[...] = jnp.sum(hub_recv[...].astype(F32), axis=0)

    drain(hub_all.at[pl.ds(0, (chips - 1) * bnd)], s_send.at[0])
    drain(recv1.at[pl.ds(0, total - 1)], s_send.at[1])
    drain(pair_in, s_send.at[2])
    drain(wpair, s_send.at[3])
    drain(bpair, s_send.at[4])
    drain(recv1.at[pl.ds(0, total - 1)], s_send.at[5])
    drain(wrecv.at[pl.ds(0, chips - 1)], s_send.at[6])
    drain(brecv.at[pl.ds(0, chips - 1)], s_send.at[7])
    drain(pair_in, s_send.at[8])
    drain(hub_recv.at[pl.ds(0, chips - 1)], s_send.at[9])
    drain(wrecv.at[pl.ds(0, chips - 1)], s_send.at[10])
    drain(wtot.at[0], s_send.at[11])
    act_copy.wait()
    gf_copy.wait()


def write_out(*refs):
    count = len(refs) // 2
    sems = refs[-1]
    copies = [
        pltpu.make_async_copy(refs[k], refs[count + k], sems.at[k]) for k in range(count)
    ]
    for copy in copies:
        copy.start()
    for copy in copies:
        copy.wait()


def solution(mesh):
    rows_n, cols_n = mesh.shape["row"], mesh.shape["col"]

    def body(
        features,
        hub_features,
        w_self,
        w_neigh,
        out_bias,
        local_edges,
        hub_edges,
        remote_edges,
        send_rows,
        cotangent,
    ):
        nodes, width = features.shape
        hub_own = hub_features.shape[0]
        total = rows_n * cols_n
        chips = total // 2
        bnd = send_rows.shape[1] // total
        hubs = hub_own * total
        fanouts = (local_edges.shape[1], hub_edges.shape[1], remote_edges.shape[1])
        vmem = pl.BlockSpec(memory_space=pltpu.VMEM)
        hbm = pl.BlockSpec(memory_space=pl.ANY)
        dma = pltpu.SemaphoreType.DMA
        outs = pl.pallas_call(
            functools.partial(kernel, rows_n, cols_n, fanouts),
            out_shape=(
                jax.ShapeDtypeStruct((nodes, width), BF16),
                jax.ShapeDtypeStruct((nodes, width), F32),
                jax.ShapeDtypeStruct((hub_own, width), F32),
                jax.ShapeDtypeStruct((width, width), F32),
                jax.ShapeDtypeStruct((width, width), F32),
                jax.ShapeDtypeStruct((1, width), F32),
            ),
            in_specs=[hbm] + [vmem] * 8 + [hbm],
            out_specs=(hbm, hbm) + (vmem,) * 4,
            scratch_shapes=[
                pltpu.VMEM((nodes, width), BF16),
                pltpu.VMEM((nodes, width), BF16),
                pltpu.VMEM((nodes, width), BF16),
                pltpu.VMEM((nodes, width), F32),
                pltpu.VMEM((nodes, width), BF16),
                pltpu.VMEM((nodes, width), BF16),
                pltpu.VMEM((16, nodes), F32),
                pltpu.VMEM((nodes, 16), F32),
                pltpu.VMEM((nodes, hubs), BF16),
                pltpu.VMEM((nodes, total * bnd), BF16),
                pltpu.VMEM((total * bnd, nodes), BF16),
                pltpu.VMEM((TILE, nodes), BF16),
                pltpu.VMEM((total, bnd, width), BF16),
                pltpu.VMEM((total, bnd, width), BF16),
                pltpu.VMEM((hubs, width), BF16),
                pltpu.VMEM((total, bnd, width), BF16),
                pltpu.VMEM((total, bnd, width), BF16),
                pltpu.VMEM((nodes, width), BF16),
                pltpu.VMEM((hubs // 2, width), BF16),
                pltpu.VMEM((hubs // 2, width), BF16),
                pltpu.VMEM((hubs // 2, width), F32),
                pltpu.VMEM((chips, hub_own, width), BF16),
                pltpu.VMEM((chips, hub_own, width), BF16),
                pltpu.VMEM((2, width, width), F32),
                pltpu.VMEM((width, width), F32),
                pltpu.VMEM((chips, 8, 128), BF16),
                pltpu.VMEM((chips, 8, 128), BF16),
                pltpu.VMEM((8, 128), BF16),
                pltpu.VMEM((2, chips, 8, 128), BF16),
                pltpu.VMEM((8, width), F32),
                pltpu.VMEM((8, width), F32),
                pltpu.VMEM((chips, 1, width), F32),
                dma((12,)),
                dma,
                dma,
                dma,
                dma((2,)),
                dma,
                dma,
                dma,
                dma,
                dma,
                dma,
                dma,
                dma((4,)),
            ],
            compiler_params=pltpu.CompilerParams(
                collective_id=0, has_side_effects=True, vmem_limit_bytes=60 << 20
            ),
        )(
            features,
            hub_features,
            w_self,
            w_neigh,
            out_bias.reshape(1, width),
            local_edges.T,
            hub_edges.T,
            remote_edges.T,
            send_rows,
            cotangent,
        )
        outs = pl.pallas_call(
            write_out,
            out_shape=tuple(jax.ShapeDtypeStruct(o.shape, o.dtype) for o in outs),
            in_specs=[hbm] * len(outs),
            out_specs=(hbm,) * len(outs),
            scratch_shapes=[dma((len(outs),))],
        )(*outs)
        activated, grad_features, grad_hubs, grad_w_self, grad_w_neigh, grad_bias = outs
        return activated, grad_features, grad_hubs, grad_w_self, grad_w_neigh, grad_bias.reshape(width)

    by_node = P(("row", "col"), None)
    return jax.shard_map(
        body,
        mesh=mesh,
        in_specs=(by_node, by_node, P(), P(), P(), by_node, by_node, by_node, by_node, by_node),
        out_specs=(by_node, by_node, by_node, P(), P(), P()),
        check_vma=False,
    )
```

```python
import functools

import jax
import jax.numpy as jnp
from jax import lax
from jax.experimental import pallas as pl
from jax.experimental.pallas import tpu as pltpu
from jax.sharding import PartitionSpec as P

MESH = pl.DeviceIdType.MESH
F32 = jnp.float32
BF16 = jnp.bfloat16
TILE = 256
BIG = 512


def kernel(
    rows_n,
    cols_n,
    fanouts,
    x_in,
    hub_ref,
    ws_ref,
    wn_ref,
    bias_ref,
    el_ref,
    eh_ref,
    er_ref,
    es_ref,
    cot_in,
    act_out,
    gf_out,
    ghub_ref,
    gws_ref,
    gwn_ref,
    gb_ref,
    x_ref,
    cot_ref,
    act_ref,
    gf_ref,
    mean_ref,
    gp_ref,
    pre_ref,
    erow,
    t_loc,
    t_hub,
    t_rem,
    t_list,
    send1,
    recv1,
    hub_all,
    send2,
    recv2,
    gm,
    pair_out,
    pair_in,
    hub_own,
    hub_send,
    hub_recv,
    wpart,
    wpair,
    wsend,
    wrecv,
    wown,
    wtot,
    bpart,
    bpair,
    brecv,
    s_send,
    s_hub,
    s_hubp,
    s_bnd,
    s_wpair,
    s_w,
    s_b,
    s_gb,
    s_gpair,
    s_ghub,
    s_wag,
    s_wagp,
    s_io,
):
    fl, fh, fr = fanouts
    fanout = fl + fh + fr
    nodes, width = x_ref.shape
    x_copy = pltpu.make_async_copy(x_in, x_ref, s_io.at[0])
    x_copy.start()
    cot_copy = pltpu.make_async_copy(cot_in, cot_ref, s_io.at[1])
    cot_copy.start()
    tiles = nodes // TILE
    bnd = send1.shape[1]
    row = lax.axis_index("row")
    col = lax.axis_index("col")
    core = lax.rem(row, 2)
    yy = row // 2
    me = row * cols_n + col
    partner = (row + 1 - 2 * core, col)
    chips = rows_n // 2 * cols_n
    total = rows_n * cols_n
    chip = yy * cols_n + col

    def far(i):
        return lax.rem(2 + 3 * i + 3 * (i // 2) + 2 * (i // 3), 4)

    order = (2, 1, 3, 0)
    zs = [lax.rem(col // 4 + dz, 4) * 4 for dz in order]
    xs = [lax.rem(col + dx, 4) for dx in order]
    far_cols = [z2 + x2 for z2 in zs for x2 in xs]

    def far_row(i):
        return lax.rem(yy + far(i // 2), 4) * 2 + lax.rem(core + 1 + i, 2)

    def each_chip(fn):
        def one_row(i, c):
            y2 = lax.rem(yy + far(i), 4)
            for c2 in far_cols:
                fn(y2, c2)
            return c

        lax.fori_loop(0, rows_n // 2 - 1, one_row, 0)
        for c2 in far_cols[:-1]:
            fn(yy, c2)

    def remote(src, dst, ssem, rsem, dev):
        return pltpu.make_async_remote_copy(
            src_ref=src, dst_ref=dst, send_sem=ssem, recv_sem=rsem, device_id=dev, device_id_type=MESH
        )

    def drain(ref, sem):
        pltpu.make_async_copy(ref, ref, sem).wait()

    barrier = pltpu.get_barrier_semaphore()

    def greet(r2, c2):
        pl.semaphore_signal(barrier, inc=1, device_id=(r2, c2), device_id_type=MESH)

    def greet_row(i, c):
        r2 = far_row(i)
        for c2 in far_cols:
            greet(r2, c2)
        return c

    lax.fori_loop(0, rows_n - 1, greet_row, 0)
    for c2 in far_cols[:-1]:
        greet(row, c2)

    erow[...] = jnp.concatenate(
        [
            el_ref[...].astype(F32),
            eh_ref[...].astype(F32),
            er_ref[...].astype(F32),
            es_ref[...].astype(F32),
            jnp.zeros((16 - fanout - 1, nodes), F32),
        ],
        axis=0,
    )
    local = range(0, fl)
    hubs = range(fl, fl + fh)
    remotes = range(fl + fh, fanout)
    lists = range(fanout, fanout + 1)

    sub_id = lax.broadcasted_iota(jnp.int32, (TILE, TILE), 0).astype(F32).astype(BF16)
    one = jnp.ones((TILE, TILE), BF16)
    zero = jnp.zeros((TILE, TILE), BF16)

    def build(dst, js):
        def strip(rb, c):
            base = (rb * TILE).astype(F32)
            for t in range(tiles):
                shifted = (erow[:, pl.ds(t * TILE, TILE)] - base).astype(BF16)
                acc = None
                for j in js:
                    hit = jnp.where(shifted[j : j + 1, :] == sub_id, one, zero)
                    acc = hit if acc is None else acc + hit
                dst[pl.ds(rb * TILE, TILE), pl.ds(t * TILE, TILE)] = acc
            return c

        lax.fori_loop(0, tiles, strip, 0)

    def dot(a, b):
        return jnp.dot(a, b, preferred_element_type=F32)

    def dot_rows(a, b):
        return lax.dot_general(a, b, (((0,), (0,)), ((), ())), preferred_element_type=F32)

    def dot_cols(a, b):
        return lax.dot_general(a, b, (((1,), (1,)), ((), ())), preferred_element_type=F32)

    build(t_list, lists)

    pl.semaphore_wait(barrier, total - 1)

    hub_all[pl.ds(me * bnd, bnd), :] = hub_ref[...]
    each_chip(
        lambda y2, c2: remote(
            hub_ref, hub_all.at[pl.ds(me * bnd, bnd)], s_send.at[0], s_hub, (y2 * 2 + core, c2)
        ).start()
    )

    def send_row(i, count, src, dst, ssem, rsem):
        r2 = far_row(i)
        for c2 in far_cols[:count]:
            remote(src.at[r2 * cols_n + c2], dst.at[me], ssem, rsem, (r2, c2)).start()

    x_copy.wait()
    send1[...] = dot_rows(t_list[...], x_ref[...]).astype(BF16).reshape(total, bnd, width)

    def send_picked(i, c):
        send_row(i, cols_n, send1, recv1, s_send.at[1], s_bnd)
        return c

    lax.fori_loop(0, rows_n - 1, send_picked, 0)
    send_row(rows_n - 1, cols_n - 1, send1, recv1, s_send.at[1], s_bnd)
    recv1[me] = send1[me]

    build(t_loc, local)
    gf_ref[...] = dot_rows(t_loc[...], x_ref[...])
    pre_ref[...] = dot(x_ref[...], ws_ref[...]) + bias_ref[...]

    drain(hub_all.at[pl.ds(0, (chips - 1) * bnd)], s_hub)
    for y2 in range(rows_n // 2):
        part = hub_all.at[pl.ds((y2 * 2 + core) * TILE, TILE)]
        remote(part, part, s_send.at[2], s_hubp, partner).start()

    build(t_hub, hubs)
    build(t_rem, remotes)
    drain(hub_all.at[pl.ds(0, rows_n // 2 * TILE)], s_hubp)

    gf_ref[...] += dot_rows(t_hub[...], hub_all[...])
    drain(recv1.at[pl.ds(0, total - 1)], s_bnd)

    cot_copy.wait()
    gf_ref[...] += dot_rows(t_rem[...], recv1[...].reshape(total * bnd, width))

    def dense(nb, c):
        rows = pl.ds(nb * BIG, BIG)
        mean = (gf_ref[rows, :] / float(fanout)).astype(BF16)
        mean_ref[rows, :] = mean
        pre = pre_ref[rows, :] + dot(mean, wn_ref[...])
        sig = jax.nn.sigmoid(pre)
        act_ref[rows, :] = (pre * sig).astype(BF16)
        gp_ref[rows, :] = (
            cot_ref[rows, :].astype(F32) * sig * (1.0 + pre * (1.0 - sig))
        ).astype(BF16)
        return c

    lax.fori_loop(0, nodes // BIG, dense, 0)
    act_copy = pltpu.make_async_copy(act_ref, act_out, s_io.at[2])
    act_copy.start()

    gm[...] = (dot_cols(gp_ref[...], wn_ref[...]) / float(fanout)).astype(BF16)

    def spread_and_send(i, c):
        y2 = lax.rem(yy + far(i), 4)
        out = dot(t_rem[pl.ds(pl.multiple_of(y2 * BIG, BIG), BIG), :], gm[...]).astype(BF16)
        send2[pl.ds(y2 * 2 * cols_n, 2 * cols_n)] = out.reshape(2 * cols_n, bnd, width)
        return c

    def spread_step(i, c):
        spread_and_send(i, 0)
        send_row(2 * i, cols_n, send2, recv2, s_send.at[5], s_gb)
        send_row(2 * i + 1, cols_n, send2, recv2, s_send.at[5], s_gb)
        return c

    lax.fori_loop(0, rows_n // 2 - 1, spread_step, 0)
    spread_and_send(jnp.int32(rows_n // 2 - 1), 0)
    send_row(rows_n - 2, cols_n, send2, recv2, s_send.at[5], s_gb)
    send_row(rows_n - 1, cols_n - 1, send2, recv2, s_send.at[5], s_gb)
    recv2[me] = send2[me]

    wpart[0] = dot_rows(x_ref[...], gp_ref[...])
    wpart[1] = dot_rows(mean_ref[...], gp_ref[...])
    bpart[0:1, :] = jnp.sum(gp_ref[...].astype(F32), axis=0, keepdims=True)
    remote(wpart.at[1 - core], wpair, s_send.at[3], s_wpair.at[0], partner).start()
    remote(bpart, bpair, s_send.at[4], s_wpair.at[1], partner).start()

    hub_own[...] = dot(t_hub[...], gm[...])
    for y2 in range(rows_n // 2):
        pair_out[pl.ds(y2 * TILE, TILE), :] = hub_own[
            pl.ds(pl.multiple_of((y2 * 2 + 1 - core) * TILE, TILE), TILE), :
        ].astype(BF16)
    remote(pair_out, pair_in, s_send.at[8], s_gpair, partner).start()

    drain(wpair, s_wpair.at[0])
    drain(bpair, s_wpair.at[1])
    both = wpart[core] + wpair[...]
    for h in range(2):
        wsend[pl.ds(h * (chips // 2), chips // 2)] = (
            both[:, h * 128 : h * 128 + 128].astype(BF16).reshape(chips // 2, 8, 128)
        )
    brecv[chip] = bpart[0:1, :] + bpair[0:1, :]

    def send_weights(y2, c2):
        dev = (y2 * 2 + core, c2)
        remote(wsend.at[y2 * cols_n + c2], wrecv.at[chip], s_send.at[6], s_w, dev).start()
        remote(brecv.at[chip], brecv.at[chip], s_send.at[7], s_b, dev).start()

    each_chip(send_weights)
    wrecv[chip] = wsend[chip]
    drain(pair_in, s_gpair)

    def hub_join(y2, c):
        rows = pl.ds(y2 * TILE, TILE)
        mine = hub_own[pl.ds((y2 * 2 + core) * TILE, TILE), :]
        both = (mine + pair_in[rows, :].astype(F32)).astype(BF16)
        hub_send[pl.ds(y2 * cols_n, cols_n)] = both.reshape(cols_n, bnd, width)
        return c

    lax.fori_loop(0, rows_n // 2, hub_join, 0)
    each_chip(
        lambda y2, c2: remote(
            hub_send.at[y2 * cols_n + c2],
            hub_recv.at[chip],
            s_send.at[9],
            s_ghub,
            (y2 * 2 + core, c2),
        ).start()
    )
    hub_recv[chip] = hub_send[chip]

    gf_ref[...] = dot_cols(gp_ref[...], ws_ref[...])
    gf_ref[...] += dot(t_loc[...], gm[...])
    drain(wrecv.at[pl.ds(0, chips - 1)], s_w)
    drain(brecv.at[pl.ds(0, chips - 1)], s_b)
    wown[...] = jnp.sum(wrecv[...].astype(F32), axis=0).astype(BF16)
    each_chip(
        lambda y2, c2: remote(
            wown, wtot.at[core, chip], s_send.at[10], s_wag, (y2 * 2 + core, c2)
        ).start()
    )
    wtot[core, chip] = wown[...]
    gb_ref[...] = jnp.sum(brecv[...], axis=0)

    drain(recv2.at[pl.ds(0, total - 1)], s_gb)

    gf_ref[...] += dot(t_list[...], recv2[...].reshape(total * bnd, width))
    gf_copy = pltpu.make_async_copy(gf_ref, gf_out, s_io.at[3])
    gf_copy.start()
    drain(wrecv.at[pl.ds(0, chips - 1)], s_wag)
    remote(wtot.at[core], wtot.at[core], s_send.at[11], s_wagp, partner).start()

    drain(hub_recv.at[pl.ds(0, chips - 1)], s_ghub)
    ghub_ref[...] = jnp.sum(hub_recv[...].astype(F32), axis=0)

    drain(wtot.at[0], s_wagp)
    for h in range(2):
        part = pl.ds(h * (chips // 2), chips // 2)
        gws_ref[:, pl.ds(h * 128, 128)] = wtot[0, part].astype(F32).reshape(width, 128)
        gwn_ref[:, pl.ds(h * 128, 128)] = wtot[1, part].astype(F32).reshape(width, 128)
    drain(hub_all.at[pl.ds(0, (chips - 1) * bnd)], s_send.at[0])
    drain(recv1.at[pl.ds(0, total - 1)], s_send.at[1])
    drain(pair_in, s_send.at[2])
    drain(wpair, s_send.at[3])
    drain(bpair, s_send.at[4])
    drain(recv1.at[pl.ds(0, total - 1)], s_send.at[5])
    drain(wrecv.at[pl.ds(0, chips - 1)], s_send.at[6])
    drain(brecv.at[pl.ds(0, chips - 1)], s_send.at[7])
    drain(pair_in, s_send.at[8])
    drain(hub_recv.at[pl.ds(0, chips - 1)], s_send.at[9])
    drain(wrecv.at[pl.ds(0, chips - 1)], s_send.at[10])
    drain(wtot.at[0], s_send.at[11])
    act_copy.wait()
    gf_copy.wait()


def write_out(pieces, *refs):
    count = len(pieces)
    sources, results, held = refs[:count], refs[count : 2 * count], refs[2 * count : 3 * count]
    arrive, leave = refs[3 * count], refs[3 * count + 1]
    steps = []
    for k, parts in enumerate(pieces):
        size = sources[k].shape[0] // parts
        for p in range(parts):
            rows = pl.ds(p * size, size)
            n = len(steps)
            steps.append(
                (
                    pltpu.make_async_copy(sources[k].at[rows], held[k].at[rows], arrive.at[n]),
                    pltpu.make_async_copy(held[k].at[rows], results[k].at[rows], leave.at[n]),
                )
            )
    for inward, outward in steps:
        inward.start()
    for inward, outward in steps:
        inward.wait()
        outward.start()
    for inward, outward in steps:
        outward.wait()


def solution(mesh):
    rows_n, cols_n = mesh.shape["row"], mesh.shape["col"]

    def body(
        features,
        hub_features,
        w_self,
        w_neigh,
        out_bias,
        local_edges,
        hub_edges,
        remote_edges,
        send_rows,
        cotangent,
    ):
        nodes, width = features.shape
        hub_own = hub_features.shape[0]
        total = rows_n * cols_n
        chips = total // 2
        bnd = send_rows.shape[1] // total
        hubs = hub_own * total
        fanouts = (local_edges.shape[1], hub_edges.shape[1], remote_edges.shape[1])
        vmem = pl.BlockSpec(memory_space=pltpu.VMEM)
        hbm = pl.BlockSpec(memory_space=pl.ANY)
        dma = pltpu.SemaphoreType.DMA
        outs = pl.pallas_call(
            functools.partial(kernel, rows_n, cols_n, fanouts),
            out_shape=(
                jax.ShapeDtypeStruct((nodes, width), BF16),
                jax.ShapeDtypeStruct((nodes, width), F32),
                jax.ShapeDtypeStruct((hub_own, width), F32),
                jax.ShapeDtypeStruct((width, width), F32),
                jax.ShapeDtypeStruct((width, width), F32),
                jax.ShapeDtypeStruct((1, width), F32),
            ),
            in_specs=[hbm] + [vmem] * 8 + [hbm],
            out_specs=(hbm, hbm) + (vmem,) * 4,
            scratch_shapes=[
                pltpu.VMEM((nodes, width), BF16),
                pltpu.VMEM((nodes, width), BF16),
                pltpu.VMEM((nodes, width), BF16),
                pltpu.VMEM((nodes, width), F32),
                pltpu.VMEM((nodes, width), BF16),
                pltpu.VMEM((nodes, width), BF16),
                pltpu.VMEM((nodes, width), F32),
                pltpu.VMEM((16, nodes), F32),
                pltpu.VMEM((nodes, nodes), BF16),
                pltpu.VMEM((hubs, nodes), BF16),
                pltpu.VMEM((total * bnd, nodes), BF16),
                pltpu.VMEM((nodes, total * bnd), BF16),
                pltpu.VMEM((total, bnd, width), BF16),
                pltpu.VMEM((total, bnd, width), BF16),
                pltpu.VMEM((hubs, width), BF16),
                pltpu.VMEM((total, bnd, width), BF16),
                pltpu.VMEM((total, bnd, width), BF16),
                pltpu.VMEM((nodes, width), BF16),
                pltpu.VMEM((hubs // 2, width), BF16),
                pltpu.VMEM((hubs // 2, width), BF16),
                pltpu.VMEM((hubs, width), F32),
                pltpu.VMEM((chips, hub_own, width), BF16),
                pltpu.VMEM((chips, hub_own, width), BF16),
                pltpu.VMEM((2, width, width), F32),
                pltpu.VMEM((width, width), F32),
                pltpu.VMEM((chips, 8, 128), BF16),
                pltpu.VMEM((chips, 8, 128), BF16),
                pltpu.VMEM((8, 128), BF16),
                pltpu.VMEM((2, chips, 8, 128), BF16),
                pltpu.VMEM((8, width), F32),
                pltpu.VMEM((8, width), F32),
                pltpu.VMEM((chips, 1, width), F32),
                dma((12,)),
                dma,
                dma,
                dma,
                dma((2,)),
                dma,
                dma,
                dma,
                dma,
                dma,
                dma,
                dma,
                dma((4,)),
            ],
            compiler_params=pltpu.CompilerParams(
                collective_id=0, has_side_effects=True, vmem_limit_bytes=60 << 20
            ),
        )(
            features,
            hub_features,
            w_self,
            w_neigh,
            out_bias.reshape(1, width),
            local_edges.T,
            hub_edges.T,
            remote_edges.T,
            send_rows,
            cotangent,
        )
        pieces = (2, 4, 1, 1, 1, 1)
        outs = pl.pallas_call(
            functools.partial(write_out, pieces),
            out_shape=tuple(jax.ShapeDtypeStruct(o.shape, o.dtype) for o in outs),
            in_specs=[hbm] * len(outs),
            out_specs=(hbm,) * len(outs),
            scratch_shapes=[pltpu.VMEM(o.shape, o.dtype) for o in outs]
            + [dma((sum(pieces),)), dma((sum(pieces),))],
        )(*outs)
        activated, grad_features, grad_hubs, grad_w_self, grad_w_neigh, grad_bias = outs
        return activated, grad_features, grad_hubs, grad_w_self, grad_w_neigh, grad_bias.reshape(width)

    by_node = P(("row", "col"), None)
    return jax.shard_map(
        body,
        mesh=mesh,
        in_specs=(by_node, by_node, P(), P(), P(), by_node, by_node, by_node, by_node, by_node),
        out_specs=(by_node, by_node, by_node, P(), P(), P()),
        check_vma=False,
    )
```

```python
import functools

import jax
import jax.numpy as jnp
from jax import lax
from jax.experimental import pallas as pl
from jax.experimental.pallas import tpu as pltpu
from jax.sharding import PartitionSpec as P

MESH = pl.DeviceIdType.MESH
F32 = jnp.float32
BF16 = jnp.bfloat16
TILE = 256
BIG = 512


def kernel(
    rows_n,
    cols_n,
    fanouts,
    x_in,
    hub_ref,
    ws_ref,
    wn_ref,
    bias_ref,
    el_ref,
    eh_ref,
    er_ref,
    es_ref,
    cot_in,
    act_out,
    gf_out,
    ghub_ref,
    gws_ref,
    gwn_ref,
    gb_ref,
    x_ref,
    cot_ref,
    act_ref,
    gf_ref,
    mean_ref,
    gp_ref,
    pre_ref,
    erow,
    t_loc,
    t_hub,
    t_rem,
    t_list,
    send1,
    recv1,
    hub_all,
    send2,
    recv2,
    gm,
    pair_out,
    pair_in,
    hub_own,
    hub_send,
    hub_recv,
    wpart,
    wpair,
    wsend,
    wrecv,
    wown,
    wtot,
    bpart,
    bpair,
    brecv,
    s_send,
    s_hub,
    s_hubp,
    s_bnd,
    s_wpair,
    s_w,
    s_b,
    s_gb,
    s_gpair,
    s_ghub,
    s_wag,
    s_wagp,
    s_io,
):
    fl, fh, fr = fanouts
    fanout = fl + fh + fr
    nodes, width = x_ref.shape
    x_copy = pltpu.make_async_copy(x_in, x_ref, s_io.at[0])
    x_copy.start()
    cot_copy = pltpu.make_async_copy(cot_in, cot_ref, s_io.at[1])
    cot_copy.start()
    tiles = nodes // TILE
    bnd = send1.shape[1]
    row = lax.axis_index("row")
    col = lax.axis_index("col")
    core = lax.rem(row, 2)
    yy = row // 2
    me = row * cols_n + col
    partner = (row + 1 - 2 * core, col)
    chips = rows_n // 2 * cols_n
    total = rows_n * cols_n
    chip = yy * cols_n + col

    def far(i):
        return lax.rem(2 + 3 * i + 3 * (i // 2) + 2 * (i // 3), 4)

    order = (2, 1, 3, 0)
    zs = [lax.rem(col // 4 + dz, 4) * 4 for dz in order]
    xs = [lax.rem(col + dx, 4) for dx in order]
    far_cols = [z2 + x2 for z2 in zs for x2 in xs]

    def far_row(i):
        return lax.rem(yy + far(i // 2), 4) * 2 + lax.rem(core + 1 + i, 2)

    def each_chip(fn):
        def one_row(i, c):
            y2 = lax.rem(yy + far(i), 4)
            for c2 in far_cols:
                fn(y2, c2)
            return c

        lax.fori_loop(0, rows_n // 2 - 1, one_row, 0)
        for c2 in far_cols[:-1]:
            fn(yy, c2)

    def remote(src, dst, ssem, rsem, dev):
        return pltpu.make_async_remote_copy(
            src_ref=src, dst_ref=dst, send_sem=ssem, recv_sem=rsem, device_id=dev, device_id_type=MESH
        )

    def drain(ref, sem):
        pltpu.make_async_copy(ref, ref, sem).wait()

    barrier = pltpu.get_barrier_semaphore()

    def greet(r2, c2):
        pl.semaphore_signal(barrier, inc=1, device_id=(r2, c2), device_id_type=MESH)

    def greet_row(i, c):
        r2 = far_row(i)
        for c2 in far_cols:
            greet(r2, c2)
        return c

    lax.fori_loop(0, rows_n - 1, greet_row, 0)
    for c2 in far_cols[:-1]:
        greet(row, c2)

    erow[...] = jnp.concatenate(
        [
            el_ref[...].astype(F32),
            eh_ref[...].astype(F32),
            er_ref[...].astype(F32),
            es_ref[...].astype(F32),
            jnp.zeros((16 - fanout - 1, nodes), F32),
        ],
        axis=0,
    )
    local = range(0, fl)
    hubs = range(fl, fl + fh)
    remotes = range(fl + fh, fanout)
    lists = range(fanout, fanout + 1)

    sub_id = lax.broadcasted_iota(jnp.int32, (TILE, TILE), 0).astype(F32).astype(BF16)
    one = jnp.ones((TILE, TILE), BF16)
    zero = jnp.zeros((TILE, TILE), BF16)

    def strip(dst, rb, js):
        base = (rb * TILE).astype(F32)
        for t in range(tiles):
            shifted = (erow[:, pl.ds(t * TILE, TILE)] - base).astype(BF16)
            acc = None
            for j in js:
                hit = jnp.where(shifted[j : j + 1, :] == sub_id, one, zero)
                acc = hit if acc is None else acc + hit
            dst[pl.ds(rb * TILE, TILE), pl.ds(t * TILE, TILE)] = acc

    def build(dst, js):
        def one_strip(rb, c):
            strip(dst, rb, js)
            return c

        lax.fori_loop(0, tiles, one_strip, 0)

    def gather_sum(out, counts, table, js=None):
        def step(kb, c):
            if js is not None:
                strip(counts, 2 * kb, js)
                strip(counts, 2 * kb + 1, js)
            rows = pl.ds(kb * BIG, BIG)
            out[...] += dot_rows(counts[rows, :], table[rows, :])
            return c

        lax.fori_loop(0, nodes // BIG, step, 0)

    def in_blocks(fn, size=BIG):
        def step(nb, c):
            fn(pl.ds(nb * size, size))
            return c

        lax.fori_loop(0, nodes // size, step, 0)

    def dot(a, b):
        return jnp.dot(a, b, preferred_element_type=F32)

    def dot_rows(a, b):
        return lax.dot_general(a, b, (((0,), (0,)), ((), ())), preferred_element_type=F32)

    def dot_cols(a, b):
        return lax.dot_general(a, b, (((1,), (1,)), ((), ())), preferred_element_type=F32)

    build(t_list, lists)
    gf_ref[...] = jnp.zeros_like(gf_ref)

    pl.semaphore_wait(barrier, total - 1)

    hub_all[pl.ds(me * bnd, bnd), :] = hub_ref[...]
    each_chip(
        lambda y2, c2: remote(
            hub_ref, hub_all.at[pl.ds(me * bnd, bnd)], s_send.at[0], s_hub, (y2 * 2 + core, c2)
        ).start()
    )

    def send_row(i, count, src, dst, ssem, rsem):
        r2 = far_row(i)
        for c2 in far_cols[:count]:
            remote(src.at[r2 * cols_n + c2], dst.at[me], ssem, rsem, (r2, c2)).start()

    x_copy.wait()
    gather_sum(gf_ref, t_list, x_ref)
    send1[...] = gf_ref[...].astype(BF16).reshape(total, bnd, width)

    def send_picked(i, c):
        send_row(i, cols_n, send1, recv1, s_send.at[1], s_bnd.at[i // 2])
        return c

    lax.fori_loop(0, rows_n - 1, send_picked, 0)
    send_row(rows_n - 1, cols_n - 1, send1, recv1, s_send.at[1], s_bnd.at[rows_n // 2 - 1])
    recv1[me] = send1[me]

    gf_ref[...] = jnp.zeros_like(gf_ref)
    gather_sum(gf_ref, t_loc, x_ref, local)

    def own_part(rows):
        pre_ref[rows, :] = dot(x_ref[rows, :], ws_ref[...]) + bias_ref[...]

    in_blocks(own_part)

    drain(hub_all.at[pl.ds(0, (chips - 1) * bnd)], s_hub)
    for y2 in range(rows_n // 2):
        part = hub_all.at[pl.ds((y2 * 2 + core) * TILE, TILE)]
        remote(part, part, s_send.at[2], s_hubp, partner).start()

    build(t_rem, remotes)
    drain(hub_all.at[pl.ds(0, rows_n // 2 * TILE)], s_hubp)

    gather_sum(gf_ref, t_hub, hub_all, hubs)

    def remote_part(i):
        y2 = lax.rem(yy + 4 - far(i), 4)
        incoming = recv1[pl.ds(y2 * 2 * cols_n, 2 * cols_n)].reshape(BIG, width)
        gf_ref[...] += dot_rows(t_rem[pl.ds(pl.multiple_of(y2 * BIG, BIG), BIG), :], incoming)

    def remote_step(i, c):
        drain(recv1.at[pl.ds(0, 2 * cols_n)], s_bnd.at[i])
        remote_part(i)
        return c

    lax.fori_loop(0, rows_n // 2 - 1, remote_step, 0)
    drain(recv1.at[pl.ds(0, 2 * cols_n - 1)], s_bnd.at[rows_n // 2 - 1])
    cot_copy.wait()
    remote_part(jnp.int32(rows_n // 2 - 1))

    def dense(rows):
        mean = (gf_ref[rows, :] / float(fanout)).astype(BF16)
        mean_ref[rows, :] = mean
        pre = pre_ref[rows, :] + dot(mean, wn_ref[...])
        sig = jax.nn.sigmoid(pre)
        act_ref[rows, :] = (pre * sig).astype(BF16)
        gp_ref[rows, :] = (
            cot_ref[rows, :].astype(F32) * sig * (1.0 + pre * (1.0 - sig))
        ).astype(BF16)

    in_blocks(dense)
    act_copy = pltpu.make_async_copy(act_ref, act_out, s_io.at[2])
    act_copy.start()


    def back_mean(rows):
        gm[rows, :] = (dot_cols(gp_ref[rows, :], wn_ref[...]) / float(fanout)).astype(BF16)

    in_blocks(back_mean)

    def spread_and_send(i, c):
        y2 = lax.rem(yy + far(i), 4)
        out = dot(t_rem[pl.ds(pl.multiple_of(y2 * BIG, BIG), BIG), :], gm[...]).astype(BF16)
        send2[pl.ds(y2 * 2 * cols_n, 2 * cols_n)] = out.reshape(2 * cols_n, bnd, width)
        return c

    def spread_step(i, c):
        spread_and_send(i, 0)
        send_row(2 * i, cols_n, send2, recv2, s_send.at[5], s_gb)
        send_row(2 * i + 1, cols_n, send2, recv2, s_send.at[5], s_gb)
        return c

    lax.fori_loop(0, rows_n // 2 - 1, spread_step, 0)
    spread_and_send(jnp.int32(rows_n // 2 - 1), 0)
    send_row(rows_n - 2, cols_n, send2, recv2, s_send.at[5], s_gb)
    send_row(rows_n - 1, cols_n - 1, send2, recv2, s_send.at[5], s_gb)
    recv2[me] = send2[me]

    wpart[...] = jnp.zeros_like(wpart)
    bpart[...] = jnp.zeros_like(bpart)

    def weight_part(rows):
        gp = gp_ref[rows, :]
        wpart[0] += dot_rows(x_ref[rows, :], gp)
        wpart[1] += dot_rows(mean_ref[rows, :], gp)
        bpart[0:1, :] += jnp.sum(gp.astype(F32), axis=0, keepdims=True)

    in_blocks(weight_part)
    remote(wpart.at[1 - core], wpair, s_send.at[3], s_wpair.at[0], partner).start()
    remote(bpart, bpair, s_send.at[4], s_wpair.at[1], partner).start()

    def hub_part(rows):
        hub_own[rows, :] = dot(t_hub[rows, :], gm[...])

    in_blocks(hub_part, 2 * BIG)
    for y2 in range(rows_n // 2):
        pair_out[pl.ds(y2 * TILE, TILE), :] = hub_own[
            pl.ds(pl.multiple_of((y2 * 2 + 1 - core) * TILE, TILE), TILE), :
        ].astype(BF16)
    remote(pair_out, pair_in, s_send.at[8], s_gpair, partner).start()

    drain(wpair, s_wpair.at[0])
    drain(bpair, s_wpair.at[1])
    both = wpart[core] + wpair[...]
    for h in range(2):
        wsend[pl.ds(h * (chips // 2), chips // 2)] = (
            both[:, h * 128 : h * 128 + 128].astype(BF16).reshape(chips // 2, 8, 128)
        )
    brecv[chip] = bpart[0:1, :] + bpair[0:1, :]

    def send_weights(y2, c2):
        dev = (y2 * 2 + core, c2)
        remote(wsend.at[y2 * cols_n + c2], wrecv.at[chip], s_send.at[6], s_w, dev).start()
        remote(brecv.at[chip], brecv.at[chip], s_send.at[7], s_b, dev).start()

    each_chip(send_weights)
    wrecv[chip] = wsend[chip]
    drain(pair_in, s_gpair)

    def hub_join(y2, c):
        rows = pl.ds(y2 * TILE, TILE)
        mine = hub_own[pl.ds((y2 * 2 + core) * TILE, TILE), :]
        both = (mine + pair_in[rows, :].astype(F32)).astype(BF16)
        hub_send[pl.ds(y2 * cols_n, cols_n)] = both.reshape(cols_n, bnd, width)
        return c

    lax.fori_loop(0, rows_n // 2, hub_join, 0)
    each_chip(
        lambda y2, c2: remote(
            hub_send.at[y2 * cols_n + c2],
            hub_recv.at[chip],
            s_send.at[9],
            s_ghub,
            (y2 * 2 + core, c2),
        ).start()
    )
    hub_recv[chip] = hub_send[chip]

    def local_back(rows):
        gf_ref[rows, :] = dot_cols(gp_ref[rows, :], ws_ref[...]) + dot(t_loc[rows, :], gm[...])

    in_blocks(local_back, 2 * BIG)
    drain(wrecv.at[pl.ds(0, chips - 1)], s_w)
    drain(brecv.at[pl.ds(0, chips - 1)], s_b)
    wown[...] = jnp.sum(wrecv[...].astype(F32), axis=0).astype(BF16)
    each_chip(
        lambda y2, c2: remote(
            wown, wtot.at[core, chip], s_send.at[10], s_wag, (y2 * 2 + core, c2)
        ).start()
    )
    wtot[core, chip] = wown[...]
    gb_ref[...] = jnp.sum(brecv[...], axis=0)

    drain(recv2.at[pl.ds(0, total - 1)], s_gb)


    def return_part(rows):
        gf_ref[rows, :] += dot(t_list[rows, :], recv2[...].reshape(total * bnd, width))

    in_blocks(return_part, 2 * BIG)
    gf_copy = pltpu.make_async_copy(gf_ref, gf_out, s_io.at[3])
    gf_copy.start()
    drain(wrecv.at[pl.ds(0, chips - 1)], s_wag)
    remote(wtot.at[core], wtot.at[core], s_send.at[11], s_wagp, partner).start()

    drain(hub_recv.at[pl.ds(0, chips - 1)], s_ghub)
    ghub_ref[...] = jnp.sum(hub_recv[...].astype(F32), axis=0)

    drain(wtot.at[0], s_wagp)
    for h in range(2):
        part = pl.ds(h * (chips // 2), chips // 2)
        gws_ref[:, pl.ds(h * 128, 128)] = wtot[0, part].astype(F32).reshape(width, 128)
        gwn_ref[:, pl.ds(h * 128, 128)] = wtot[1, part].astype(F32).reshape(width, 128)
    drain(hub_all.at[pl.ds(0, (chips - 1) * bnd)], s_send.at[0])
    drain(recv1.at[pl.ds(0, total - 1)], s_send.at[1])
    drain(pair_in, s_send.at[2])
    drain(wpair, s_send.at[3])
    drain(bpair, s_send.at[4])
    drain(recv1.at[pl.ds(0, total - 1)], s_send.at[5])
    drain(wrecv.at[pl.ds(0, chips - 1)], s_send.at[6])
    drain(brecv.at[pl.ds(0, chips - 1)], s_send.at[7])
    drain(pair_in, s_send.at[8])
    drain(hub_recv.at[pl.ds(0, chips - 1)], s_send.at[9])
    drain(wrecv.at[pl.ds(0, chips - 1)], s_send.at[10])
    drain(wtot.at[0], s_send.at[11])
    act_copy.wait()
    gf_copy.wait()


def write_out(pieces, *refs):
    count = len(pieces)
    sources, results, held = refs[:count], refs[count : 2 * count], refs[2 * count : 3 * count]
    arrive, leave = refs[3 * count], refs[3 * count + 1]
    steps = []
    for k, parts in enumerate(pieces):
        size = sources[k].shape[0] // parts
        for p in range(parts):
            rows = pl.ds(p * size, size)
            n = len(steps)
            steps.append(
                (
                    pltpu.make_async_copy(sources[k].at[rows], held[k].at[rows], arrive.at[n]),
                    pltpu.make_async_copy(held[k].at[rows], results[k].at[rows], leave.at[n]),
                )
            )
    for inward, outward in steps:
        inward.start()
    for inward, outward in steps:
        inward.wait()
        outward.start()
    for inward, outward in steps:
        outward.wait()


def solution(mesh):
    rows_n, cols_n = mesh.shape["row"], mesh.shape["col"]

    def body(
        features,
        hub_features,
        w_self,
        w_neigh,
        out_bias,
        local_edges,
        hub_edges,
        remote_edges,
        send_rows,
        cotangent,
    ):
        nodes, width = features.shape
        hub_own = hub_features.shape[0]
        total = rows_n * cols_n
        chips = total // 2
        bnd = send_rows.shape[1] // total
        hubs = hub_own * total
        fanouts = (local_edges.shape[1], hub_edges.shape[1], remote_edges.shape[1])
        vmem = pl.BlockSpec(memory_space=pltpu.VMEM)
        hbm = pl.BlockSpec(memory_space=pl.ANY)
        dma = pltpu.SemaphoreType.DMA
        outs = pl.pallas_call(
            functools.partial(kernel, rows_n, cols_n, fanouts),
            out_shape=(
                jax.ShapeDtypeStruct((nodes, width), BF16),
                jax.ShapeDtypeStruct((nodes, width), F32),
                jax.ShapeDtypeStruct((hub_own, width), F32),
                jax.ShapeDtypeStruct((width, width), F32),
                jax.ShapeDtypeStruct((width, width), F32),
                jax.ShapeDtypeStruct((1, width), F32),
            ),
            in_specs=[hbm] + [vmem] * 8 + [hbm],
            out_specs=(hbm, hbm) + (vmem,) * 4,
            scratch_shapes=[
                pltpu.VMEM((nodes, width), BF16),
                pltpu.VMEM((nodes, width), BF16),
                pltpu.VMEM((nodes, width), BF16),
                pltpu.VMEM((nodes, width), F32),
                pltpu.VMEM((nodes, width), BF16),
                pltpu.VMEM((nodes, width), BF16),
                pltpu.VMEM((nodes, width), F32),
                pltpu.VMEM((16, nodes), F32),
                pltpu.VMEM((nodes, nodes), BF16),
                pltpu.VMEM((hubs, nodes), BF16),
                pltpu.VMEM((total * bnd, nodes), BF16),
                pltpu.VMEM((nodes, total * bnd), BF16),
                pltpu.VMEM((total, bnd, width), BF16),
                pltpu.VMEM((total, bnd, width), BF16),
                pltpu.VMEM((hubs, width), BF16),
                pltpu.VMEM((total, bnd, width), BF16),
                pltpu.VMEM((total, bnd, width), BF16),
                pltpu.VMEM((nodes, width), BF16),
                pltpu.VMEM((hubs // 2, width), BF16),
                pltpu.VMEM((hubs // 2, width), BF16),
                pltpu.VMEM((hubs, width), F32),
                pltpu.VMEM((chips, hub_own, width), BF16),
                pltpu.VMEM((chips, hub_own, width), BF16),
                pltpu.VMEM((2, width, width), F32),
                pltpu.VMEM((width, width), F32),
                pltpu.VMEM((chips, 8, 128), BF16),
                pltpu.VMEM((chips, 8, 128), BF16),
                pltpu.VMEM((8, 128), BF16),
                pltpu.VMEM((2, chips, 8, 128), BF16),
                pltpu.VMEM((8, width), F32),
                pltpu.VMEM((8, width), F32),
                pltpu.VMEM((chips, 1, width), F32),
                dma((12,)),
                dma,
                dma,
                dma((rows_n // 2,)),
                dma((2,)),
                dma,
                dma,
                dma,
                dma,
                dma,
                dma,
                dma,
                dma((4,)),
            ],
            compiler_params=pltpu.CompilerParams(
                collective_id=0, has_side_effects=True, vmem_limit_bytes=60 << 20
            ),
        )(
            features,
            hub_features,
            w_self,
            w_neigh,
            out_bias.reshape(1, width),
            local_edges.T,
            hub_edges.T,
            remote_edges.T,
            send_rows,
            cotangent,
        )
        pieces = (2, 4, 1, 1, 1, 1)
        outs = pl.pallas_call(
            functools.partial(write_out, pieces),
            out_shape=tuple(jax.ShapeDtypeStruct(o.shape, o.dtype) for o in outs),
            in_specs=[hbm] * len(outs),
            out_specs=(hbm,) * len(outs),
            scratch_shapes=[pltpu.VMEM(o.shape, o.dtype) for o in outs]
            + [dma((sum(pieces),)), dma((sum(pieces),))],
        )(*outs)
        activated, grad_features, grad_hubs, grad_w_self, grad_w_neigh, grad_bias = outs
        return activated, grad_features, grad_hubs, grad_w_self, grad_w_neigh, grad_bias.reshape(width)

    by_node = P(("row", "col"), None)
    return jax.shard_map(
        body,
        mesh=mesh,
        in_specs=(by_node, by_node, P(), P(), P(), by_node, by_node, by_node, by_node, by_node),
        out_specs=(by_node, by_node, by_node, P(), P(), P()),
        check_vma=False,
    )
```

```python
import functools

import jax
import jax.numpy as jnp
from jax import lax
from jax.experimental import pallas as pl
from jax.experimental.pallas import tpu as pltpu
from jax.sharding import PartitionSpec as P

MESH = pl.DeviceIdType.MESH
F32 = jnp.float32
BF16 = jnp.bfloat16
TILE = 256
BIG = 512


def kernel(
    rows_n,
    cols_n,
    fanouts,
    x_in,
    hub_in,
    ws_in,
    wn_in,
    bias_in,
    el_in,
    eh_in,
    er_in,
    es_in,
    cot_in,
    act_out,
    gf_out,
    ghub_ref,
    gws_ref,
    gwn_ref,
    gb_ref,
    hub_ref,
    ws_ref,
    wn_ref,
    bias_ref,
    el_ref,
    eh_ref,
    er_ref,
    es_ref,
    x_ref,
    cot_ref,
    act_ref,
    gf_ref,
    mean_ref,
    gp_ref,
    pre_ref,
    erow,
    t_loc,
    t_hub,
    t_rem,
    t_list,
    send1,
    recv1,
    hub_all,
    send2,
    recv2,
    gm,
    pair_out,
    pair_in,
    hub_own,
    hub_send,
    hub_recv,
    wpart,
    wpair,
    wsend,
    wrecv,
    wown,
    wtot,
    bpart,
    bpair,
    brecv,
    s_send,
    s_hub,
    s_hubp,
    s_bnd,
    s_wpair,
    s_w,
    s_b,
    s_gb,
    s_gpair,
    s_ghub,
    s_wag,
    s_wagp,
    s_io,
):
    fl, fh, fr = fanouts
    fanout = fl + fh + fr
    nodes, width = x_ref.shape
    x_copy = pltpu.make_async_copy(x_in, x_ref, s_io.at[0])
    x_copy.start()
    cot_copy = pltpu.make_async_copy(cot_in, cot_ref, s_io.at[1])
    cot_copy.start()
    small = [
        pltpu.make_async_copy(source, held, s_io.at[4 + k])
        for k, (source, held) in enumerate(
            (
                (el_in, el_ref),
                (eh_in, eh_ref),
                (er_in, er_ref),
                (es_in, es_ref),
                (hub_in, hub_ref),
                (ws_in, ws_ref),
                (wn_in, wn_ref),
                (bias_in, bias_ref),
            )
        )
    ]
    for copy in small:
        copy.start()
    tiles = nodes // TILE
    bnd = send1.shape[1]
    row = lax.axis_index("row")
    col = lax.axis_index("col")
    core = lax.rem(row, 2)
    yy = row // 2
    me = row * cols_n + col
    partner = (row + 1 - 2 * core, col)
    chips = rows_n // 2 * cols_n
    total = rows_n * cols_n
    chip = yy * cols_n + col

    def far(i):
        return lax.rem(2 + 3 * i + 3 * (i // 2) + 2 * (i // 3), 4)

    order = (2, 1, 3, 0)
    zs = [lax.rem(col // 4 + dz, 4) * 4 for dz in order]
    xs = [lax.rem(col + dx, 4) for dx in order]
    far_cols = [z2 + x2 for z2 in zs for x2 in xs]

    def far_row(i):
        return lax.rem(yy + far(i // 2), 4) * 2 + lax.rem(core + 1 + i, 2)

    def each_chip(fn):
        def one_row(i, c):
            y2 = lax.rem(yy + far(i), 4)
            for c2 in far_cols:
                fn(y2, c2)
            return c

        lax.fori_loop(0, rows_n // 2 - 1, one_row, 0)
        for c2 in far_cols[:-1]:
            fn(yy, c2)

    def remote(src, dst, ssem, rsem, dev):
        return pltpu.make_async_remote_copy(
            src_ref=src, dst_ref=dst, send_sem=ssem, recv_sem=rsem, device_id=dev, device_id_type=MESH
        )

    def drain(ref, sem):
        pltpu.make_async_copy(ref, ref, sem).wait()

    barrier = pltpu.get_barrier_semaphore()

    def greet(r2, c2):
        pl.semaphore_signal(barrier, inc=1, device_id=(r2, c2), device_id_type=MESH)

    def greet_row(i, c):
        r2 = far_row(i)
        for c2 in far_cols:
            greet(r2, c2)
        return c

    lax.fori_loop(0, rows_n - 1, greet_row, 0)
    for c2 in far_cols[:-1]:
        greet(row, c2)

    for copy in small:
        copy.wait()
    erow[...] = jnp.concatenate(
        [
            el_ref[...].astype(F32),
            eh_ref[...].astype(F32),
            er_ref[...].astype(F32),
            es_ref[...].astype(F32),
            jnp.zeros((16 - fanout - 1, nodes), F32),
        ],
        axis=0,
    )
    local = range(0, fl)
    hubs = range(fl, fl + fh)
    remotes = range(fl + fh, fanout)
    lists = range(fanout, fanout + 1)

    sub_id = lax.broadcasted_iota(jnp.int32, (TILE, TILE), 0).astype(F32).astype(BF16)
    one = jnp.ones((TILE, TILE), BF16)
    zero = jnp.zeros((TILE, TILE), BF16)

    def strip(dst, rb, js):
        base = (rb * TILE).astype(F32)
        for t in range(tiles):
            shifted = (erow[:, pl.ds(t * TILE, TILE)] - base).astype(BF16)
            acc = None
            for j in js:
                hit = jnp.where(shifted[j : j + 1, :] == sub_id, one, zero)
                acc = hit if acc is None else acc + hit
            dst[pl.ds(rb * TILE, TILE), pl.ds(t * TILE, TILE)] = acc

    def build(dst, js):
        def one_strip(rb, c):
            strip(dst, rb, js)
            return c

        lax.fori_loop(0, tiles, one_strip, 0)

    def gather_sum(out, counts, table, js=None):
        def step(kb, c):
            if js is not None:
                strip(counts, 2 * kb, js)
                strip(counts, 2 * kb + 1, js)
            rows = pl.ds(kb * BIG, BIG)
            out[...] += dot_rows(counts[rows, :], table[rows, :])
            return c

        lax.fori_loop(0, nodes // BIG, step, 0)

    def in_blocks(fn, size=BIG):
        def step(nb, c):
            fn(pl.ds(nb * size, size))
            return c

        lax.fori_loop(0, nodes // size, step, 0)

    def dot(a, b):
        return jnp.dot(a, b, preferred_element_type=F32)

    def dot_rows(a, b):
        return lax.dot_general(a, b, (((0,), (0,)), ((), ())), preferred_element_type=F32)

    def dot_cols(a, b):
        return lax.dot_general(a, b, (((1,), (1,)), ((), ())), preferred_element_type=F32)

    build(t_list, lists)
    gf_ref[...] = jnp.zeros_like(gf_ref)

    pl.semaphore_wait(barrier, total - 1)

    hub_all[pl.ds(me * bnd, bnd), :] = hub_ref[...]
    each_chip(
        lambda y2, c2: remote(
            hub_ref, hub_all.at[pl.ds(me * bnd, bnd)], s_send.at[0], s_hub, (y2 * 2 + core, c2)
        ).start()
    )

    def send_row(i, count, src, dst, ssem, rsem):
        r2 = far_row(i)
        for c2 in far_cols[:count]:
            remote(src.at[r2 * cols_n + c2], dst.at[me], ssem, rsem, (r2, c2)).start()

    x_copy.wait()
    gather_sum(gf_ref, t_list, x_ref)
    send1[...] = gf_ref[...].astype(BF16).reshape(total, bnd, width)

    def send_picked(i, c):
        send_row(i, cols_n, send1, recv1, s_send.at[1], s_bnd.at[i // 2])
        return c

    lax.fori_loop(0, rows_n - 1, send_picked, 0)
    send_row(rows_n - 1, cols_n - 1, send1, recv1, s_send.at[1], s_bnd.at[rows_n // 2 - 1])
    recv1[me] = send1[me]

    gf_ref[...] = jnp.zeros_like(gf_ref)
    gather_sum(gf_ref, t_loc, x_ref, local)

    def own_part(rows):
        pre_ref[rows, :] = dot(x_ref[rows, :], ws_ref[...]) + bias_ref[...]

    in_blocks(own_part)

    drain(hub_all.at[pl.ds(0, (chips - 1) * bnd)], s_hub)
    for y2 in range(rows_n // 2):
        part = hub_all.at[pl.ds((y2 * 2 + core) * TILE, TILE)]
        remote(part, part, s_send.at[2], s_hubp, partner).start()

    build(t_rem, remotes)
    drain(hub_all.at[pl.ds(0, rows_n // 2 * TILE)], s_hubp)

    gather_sum(gf_ref, t_hub, hub_all, hubs)

    def remote_part(i):
        y2 = lax.rem(yy + 4 - far(i), 4)
        incoming = recv1[pl.ds(y2 * 2 * cols_n, 2 * cols_n)].reshape(BIG, width)
        gf_ref[...] += dot_rows(t_rem[pl.ds(pl.multiple_of(y2 * BIG, BIG), BIG), :], incoming)

    def remote_step(i, c):
        drain(recv1.at[pl.ds(0, 2 * cols_n)], s_bnd.at[i])
        remote_part(i)
        return c

    lax.fori_loop(0, rows_n // 2 - 1, remote_step, 0)
    drain(recv1.at[pl.ds(0, 2 * cols_n - 1)], s_bnd.at[rows_n // 2 - 1])
    cot_copy.wait()
    remote_part(jnp.int32(rows_n // 2 - 1))

    def dense(rows):
        mean = (gf_ref[rows, :] / float(fanout)).astype(BF16)
        mean_ref[rows, :] = mean
        pre = pre_ref[rows, :] + dot(mean, wn_ref[...])
        sig = jax.nn.sigmoid(pre)
        act_ref[rows, :] = (pre * sig).astype(BF16)
        gp_ref[rows, :] = (
            cot_ref[rows, :].astype(F32) * sig * (1.0 + pre * (1.0 - sig))
        ).astype(BF16)

    in_blocks(dense)
    act_copy = pltpu.make_async_copy(act_ref, act_out, s_io.at[2])
    act_copy.start()


    def back_mean(rows):
        gm[rows, :] = (dot_cols(gp_ref[rows, :], wn_ref[...]) / float(fanout)).astype(BF16)

    in_blocks(back_mean)

    def spread_and_send(i, c):
        y2 = lax.rem(yy + far(i), 4)
        out = dot(t_rem[pl.ds(pl.multiple_of(y2 * BIG, BIG), BIG), :], gm[...]).astype(BF16)
        send2[pl.ds(y2 * 2 * cols_n, 2 * cols_n)] = out.reshape(2 * cols_n, bnd, width)
        return c

    def spread_step(i, c):
        spread_and_send(i, 0)
        send_row(2 * i, cols_n, send2, recv2, s_send.at[5], s_gb)
        send_row(2 * i + 1, cols_n, send2, recv2, s_send.at[5], s_gb)
        return c

    lax.fori_loop(0, rows_n // 2 - 1, spread_step, 0)
    spread_and_send(jnp.int32(rows_n // 2 - 1), 0)
    send_row(rows_n - 2, cols_n, send2, recv2, s_send.at[5], s_gb)
    send_row(rows_n - 1, cols_n - 1, send2, recv2, s_send.at[5], s_gb)
    recv2[me] = send2[me]

    wpart[...] = jnp.zeros_like(wpart)
    bpart[...] = jnp.zeros_like(bpart)

    def weight_part(rows):
        gp = gp_ref[rows, :]
        wpart[0] += dot_rows(x_ref[rows, :], gp)
        wpart[1] += dot_rows(mean_ref[rows, :], gp)
        bpart[0:1, :] += jnp.sum(gp.astype(F32), axis=0, keepdims=True)

    in_blocks(weight_part)
    remote(wpart.at[1 - core], wpair, s_send.at[3], s_wpair.at[0], partner).start()
    remote(bpart, bpair, s_send.at[4], s_wpair.at[1], partner).start()

    def hub_part(rows):
        hub_own[rows, :] = dot(t_hub[rows, :], gm[...])

    in_blocks(hub_part, 2 * BIG)
    for y2 in range(rows_n // 2):
        pair_out[pl.ds(y2 * TILE, TILE), :] = hub_own[
            pl.ds(pl.multiple_of((y2 * 2 + 1 - core) * TILE, TILE), TILE), :
        ].astype(BF16)
    remote(pair_out, pair_in, s_send.at[8], s_gpair, partner).start()

    drain(wpair, s_wpair.at[0])
    drain(bpair, s_wpair.at[1])
    both = wpart[core] + wpair[...]
    for h in range(2):
        wsend[pl.ds(h * (chips // 2), chips // 2)] = (
            both[:, h * 128 : h * 128 + 128].astype(BF16).reshape(chips // 2, 8, 128)
        )
    brecv[chip] = bpart[0:1, :] + bpair[0:1, :]

    def send_weights(y2, c2):
        dev = (y2 * 2 + core, c2)
        remote(wsend.at[y2 * cols_n + c2], wrecv.at[chip], s_send.at[6], s_w, dev).start()
        remote(brecv.at[chip], brecv.at[chip], s_send.at[7], s_b, dev).start()

    each_chip(send_weights)
    wrecv[chip] = wsend[chip]
    drain(pair_in, s_gpair)

    def hub_join(y2, c):
        rows = pl.ds(y2 * TILE, TILE)
        mine = hub_own[pl.ds((y2 * 2 + core) * TILE, TILE), :]
        both = (mine + pair_in[rows, :].astype(F32)).astype(BF16)
        hub_send[pl.ds(y2 * cols_n, cols_n)] = both.reshape(cols_n, bnd, width)
        return c

    lax.fori_loop(0, rows_n // 2, hub_join, 0)
    each_chip(
        lambda y2, c2: remote(
            hub_send.at[y2 * cols_n + c2],
            hub_recv.at[chip],
            s_send.at[9],
            s_ghub,
            (y2 * 2 + core, c2),
        ).start()
    )
    hub_recv[chip] = hub_send[chip]

    def local_back(rows):
        gf_ref[rows, :] = dot_cols(gp_ref[rows, :], ws_ref[...]) + dot(t_loc[rows, :], gm[...])

    in_blocks(local_back, 2 * BIG)
    drain(wrecv.at[pl.ds(0, chips - 1)], s_w)
    drain(brecv.at[pl.ds(0, chips - 1)], s_b)
    wown[...] = jnp.sum(wrecv[...].astype(F32), axis=0).astype(BF16)
    each_chip(
        lambda y2, c2: remote(
            wown, wtot.at[core, chip], s_send.at[10], s_wag, (y2 * 2 + core, c2)
        ).start()
    )
    wtot[core, chip] = wown[...]
    gb_ref[...] = jnp.sum(brecv[...], axis=0)

    drain(recv2.at[pl.ds(0, total - 1)], s_gb)


    def return_part(rows):
        gf_ref[rows, :] += dot(t_list[rows, :], recv2[...].reshape(total * bnd, width))

    in_blocks(return_part, 2 * BIG)
    gf_copy = pltpu.make_async_copy(gf_ref, gf_out, s_io.at[3])
    gf_copy.start()
    drain(wrecv.at[pl.ds(0, chips - 1)], s_wag)
    remote(wtot.at[core], wtot.at[core], s_send.at[11], s_wagp, partner).start()

    drain(hub_recv.at[pl.ds(0, chips - 1)], s_ghub)
    ghub_ref[...] = jnp.sum(hub_recv[...].astype(F32), axis=0)

    drain(wtot.at[0], s_wagp)
    for h in range(2):
        part = pl.ds(h * (chips // 2), chips // 2)
        gws_ref[:, pl.ds(h * 128, 128)] = wtot[0, part].astype(F32).reshape(width, 128)
        gwn_ref[:, pl.ds(h * 128, 128)] = wtot[1, part].astype(F32).reshape(width, 128)
    drain(hub_all.at[pl.ds(0, (chips - 1) * bnd)], s_send.at[0])
    drain(recv1.at[pl.ds(0, total - 1)], s_send.at[1])
    drain(pair_in, s_send.at[2])
    drain(wpair, s_send.at[3])
    drain(bpair, s_send.at[4])
    drain(recv1.at[pl.ds(0, total - 1)], s_send.at[5])
    drain(wrecv.at[pl.ds(0, chips - 1)], s_send.at[6])
    drain(brecv.at[pl.ds(0, chips - 1)], s_send.at[7])
    drain(pair_in, s_send.at[8])
    drain(hub_recv.at[pl.ds(0, chips - 1)], s_send.at[9])
    drain(wrecv.at[pl.ds(0, chips - 1)], s_send.at[10])
    drain(wtot.at[0], s_send.at[11])
    act_copy.wait()
    gf_copy.wait()


def write_out(pieces, *refs):
    count = len(pieces)
    sources, results, held = refs[:count], refs[count : 2 * count], refs[2 * count : 3 * count]
    arrive, leave = refs[3 * count], refs[3 * count + 1]
    steps = []
    for k, parts in enumerate(pieces):
        size = sources[k].shape[0] // parts
        for p in range(parts):
            rows = pl.ds(p * size, size)
            n = len(steps)
            steps.append(
                (
                    pltpu.make_async_copy(sources[k].at[rows], held[k].at[rows], arrive.at[n]),
                    pltpu.make_async_copy(held[k].at[rows], results[k].at[rows], leave.at[n]),
                )
            )
    for inward, outward in steps:
        inward.start()
    for inward, outward in steps:
        inward.wait()
        outward.start()
    for inward, outward in steps:
        outward.wait()


def solution(mesh):
    rows_n, cols_n = mesh.shape["row"], mesh.shape["col"]

    def body(
        features,
        hub_features,
        w_self,
        w_neigh,
        out_bias,
        local_edges,
        hub_edges,
        remote_edges,
        send_rows,
        cotangent,
    ):
        nodes, width = features.shape
        hub_own = hub_features.shape[0]
        total = rows_n * cols_n
        chips = total // 2
        bnd = send_rows.shape[1] // total
        hubs = hub_own * total
        fanouts = (local_edges.shape[1], hub_edges.shape[1], remote_edges.shape[1])
        vmem = pl.BlockSpec(memory_space=pltpu.VMEM)
        hbm = pl.BlockSpec(memory_space=pl.ANY)
        dma = pltpu.SemaphoreType.DMA
        outs = pl.pallas_call(
            functools.partial(kernel, rows_n, cols_n, fanouts),
            out_shape=(
                jax.ShapeDtypeStruct((nodes, width), BF16),
                jax.ShapeDtypeStruct((nodes, width), F32),
                jax.ShapeDtypeStruct((hub_own, width), F32),
                jax.ShapeDtypeStruct((width, width), F32),
                jax.ShapeDtypeStruct((width, width), F32),
                jax.ShapeDtypeStruct((1, width), F32),
            ),
            in_specs=[hbm] * 10,
            out_specs=(hbm, hbm) + (vmem,) * 4,
            scratch_shapes=[
                pltpu.VMEM((hub_own, width), BF16),
                pltpu.VMEM((width, width), BF16),
                pltpu.VMEM((width, width), BF16),
                pltpu.VMEM((1, width), F32),
                pltpu.VMEM((fanouts[0], nodes), jnp.int32),
                pltpu.VMEM((fanouts[1], nodes), jnp.int32),
                pltpu.VMEM((fanouts[2], nodes), jnp.int32),
                pltpu.VMEM((1, send_rows.shape[1]), jnp.int32),
                pltpu.VMEM((nodes, width), BF16),
                pltpu.VMEM((nodes, width), BF16),
                pltpu.VMEM((nodes, width), BF16),
                pltpu.VMEM((nodes, width), F32),
                pltpu.VMEM((nodes, width), BF16),
                pltpu.VMEM((nodes, width), BF16),
                pltpu.VMEM((nodes, width), F32),
                pltpu.VMEM((16, nodes), F32),
                pltpu.VMEM((nodes, nodes), BF16),
                pltpu.VMEM((hubs, nodes), BF16),
                pltpu.VMEM((total * bnd, nodes), BF16),
                pltpu.VMEM((nodes, total * bnd), BF16),
                pltpu.VMEM((total, bnd, width), BF16),
                pltpu.VMEM((total, bnd, width), BF16),
                pltpu.VMEM((hubs, width), BF16),
                pltpu.VMEM((total, bnd, width), BF16),
                pltpu.VMEM((total, bnd, width), BF16),
                pltpu.VMEM((nodes, width), BF16),
                pltpu.VMEM((hubs // 2, width), BF16),
                pltpu.VMEM((hubs // 2, width), BF16),
                pltpu.VMEM((hubs, width), F32),
                pltpu.VMEM((chips, hub_own, width), BF16),
                pltpu.VMEM((chips, hub_own, width), BF16),
                pltpu.VMEM((2, width, width), F32),
                pltpu.VMEM((width, width), F32),
                pltpu.VMEM((chips, 8, 128), BF16),
                pltpu.VMEM((chips, 8, 128), BF16),
                pltpu.VMEM((8, 128), BF16),
                pltpu.VMEM((2, chips, 8, 128), BF16),
                pltpu.VMEM((8, width), F32),
                pltpu.VMEM((8, width), F32),
                pltpu.VMEM((chips, 1, width), F32),
                dma((12,)),
                dma,
                dma,
                dma((rows_n // 2,)),
                dma((2,)),
                dma,
                dma,
                dma,
                dma,
                dma,
                dma,
                dma,
                dma((12,)),
            ],
            compiler_params=pltpu.CompilerParams(
                collective_id=0, has_side_effects=True, vmem_limit_bytes=60 << 20
            ),
        )(
            features,
            hub_features,
            w_self,
            w_neigh,
            out_bias.reshape(1, width),
            local_edges.T,
            hub_edges.T,
            remote_edges.T,
            send_rows,
            cotangent,
        )
        pieces = (2, 4, 1, 1, 1, 1)
        outs = pl.pallas_call(
            functools.partial(write_out, pieces),
            out_shape=tuple(jax.ShapeDtypeStruct(o.shape, o.dtype) for o in outs),
            in_specs=[hbm] * len(outs),
            out_specs=(hbm,) * len(outs),
            scratch_shapes=[pltpu.VMEM(o.shape, o.dtype) for o in outs]
            + [dma((sum(pieces),)), dma((sum(pieces),))],
        )(*outs)
        activated, grad_features, grad_hubs, grad_w_self, grad_w_neigh, grad_bias = outs
        return activated, grad_features, grad_hubs, grad_w_self, grad_w_neigh, grad_bias.reshape(width)

    by_node = P(("row", "col"), None)
    return jax.shard_map(
        body,
        mesh=mesh,
        in_specs=(by_node, by_node, P(), P(), P(), by_node, by_node, by_node, by_node, by_node),
        out_specs=(by_node, by_node, by_node, P(), P(), P()),
        check_vma=False,
    )
```

```python
import functools

import jax
import jax.numpy as jnp
from jax import lax
from jax.experimental import pallas as pl
from jax.experimental.pallas import tpu as pltpu
from jax.sharding import PartitionSpec as P

MESH = pl.DeviceIdType.MESH
F32 = jnp.float32
BF16 = jnp.bfloat16
TILE = 256
BIG = 512


def kernel(
    rows_n,
    cols_n,
    fanouts,
    x_in,
    hub_in,
    ws_in,
    wn_in,
    bias_in,
    el_in,
    eh_in,
    er_in,
    es_in,
    cot_in,
    act_out,
    gf_out,
    ghub_ref,
    gws_ref,
    gwn_ref,
    gb_ref,
    hub_ref,
    ws_ref,
    wn_ref,
    bias_ref,
    el_ref,
    eh_ref,
    er_ref,
    es_ref,
    x_ref,
    cot_ref,
    act_ref,
    gf_ref,
    mean_ref,
    gp_ref,
    pre_ref,
    erow,
    t_loc,
    t_hub,
    t_rem,
    t_list,
    send1,
    recv1,
    hub_all,
    send2,
    recv2,
    gm,
    pair_out,
    pair_in,
    hub_own,
    hub_send,
    hub_recv,
    wpart,
    wpair,
    wsend,
    wrecv,
    wown,
    wtot,
    bpart,
    bpair,
    brecv,
    s_send,
    s_hub,
    s_hubp,
    s_bnd,
    s_wpair,
    s_w,
    s_b,
    s_gb,
    s_gpair,
    s_ghub,
    s_wag,
    s_wagp,
    s_io,
):
    fl, fh, fr = fanouts
    fanout = fl + fh + fr
    nodes, width = x_ref.shape
    x_copy = pltpu.make_async_copy(x_in, x_ref, s_io.at[0])
    x_copy.start()
    cot_copy = pltpu.make_async_copy(cot_in, cot_ref, s_io.at[1])
    cot_copy.start()
    small = [
        pltpu.make_async_copy(source, held, s_io.at[4 + k])
        for k, (source, held) in enumerate(
            (
                (el_in, el_ref),
                (eh_in, eh_ref),
                (er_in, er_ref),
                (es_in, es_ref),
                (hub_in, hub_ref),
                (ws_in, ws_ref),
                (wn_in, wn_ref),
                (bias_in, bias_ref),
            )
        )
    ]
    for copy in small:
        copy.start()
    tiles = nodes // TILE
    bnd = send1.shape[1]
    row = lax.axis_index("row")
    col = lax.axis_index("col")
    core = lax.rem(row, 2)
    yy = row // 2
    me = row * cols_n + col
    partner = (row + 1 - 2 * core, col)
    chips = rows_n // 2 * cols_n
    total = rows_n * cols_n
    chip = yy * cols_n + col

    def far(i):
        return lax.rem(2 + 3 * i + 3 * (i // 2) + 2 * (i // 3), 4)

    order = (2, 1, 3, 0)
    zs = [lax.rem(col // 4 + dz, 4) * 4 for dz in order]
    xs = [lax.rem(col + dx, 4) for dx in order]
    far_cols = [z2 + x2 for z2 in zs for x2 in xs]

    def far_row(i):
        return lax.rem(yy + far(i // 2), 4) * 2 + lax.rem(core + 1 + i, 2)

    def each_chip(fn):
        def one_row(i, c):
            y2 = lax.rem(yy + far(i), 4)
            for c2 in far_cols:
                fn(y2, c2)
            return c

        lax.fori_loop(0, rows_n // 2 - 1, one_row, 0)
        for c2 in far_cols[:-1]:
            fn(yy, c2)

    def remote(src, dst, ssem, rsem, dev):
        return pltpu.make_async_remote_copy(
            src_ref=src, dst_ref=dst, send_sem=ssem, recv_sem=rsem, device_id=dev, device_id_type=MESH
        )

    def drain(ref, sem):
        pltpu.make_async_copy(ref, ref, sem).wait()

    barrier = pltpu.get_barrier_semaphore()

    def greet(r2, c2):
        pl.semaphore_signal(barrier, inc=1, device_id=(r2, c2), device_id_type=MESH)

    def greet_row(i, c):
        r2 = far_row(i)
        for c2 in far_cols:
            greet(r2, c2)
        return c

    lax.fori_loop(0, rows_n - 1, greet_row, 0)
    for c2 in far_cols[:-1]:
        greet(row, c2)

    for copy in small:
        copy.wait()
    erow[...] = jnp.concatenate(
        [
            el_ref[...].astype(F32),
            eh_ref[...].astype(F32),
            er_ref[...].astype(F32),
            es_ref[...].astype(F32),
            jnp.zeros((16 - fanout - 1, nodes), F32),
        ],
        axis=0,
    )
    local = range(0, fl)
    hubs = range(fl, fl + fh)
    remotes = range(fl + fh, fanout)
    lists = range(fanout, fanout + 1)

    sub_id = lax.broadcasted_iota(jnp.int32, (TILE, TILE), 0).astype(F32).astype(BF16)
    one = jnp.ones((TILE, TILE), BF16)
    zero = jnp.zeros((TILE, TILE), BF16)

    def strip(dst, rb, js):
        base = (rb * TILE).astype(F32)
        for t in range(tiles):
            shifted = (erow[:, pl.ds(t * TILE, TILE)] - base).astype(BF16)
            acc = None
            for j in js:
                hit = jnp.where(shifted[j : j + 1, :] == sub_id, one, zero)
                acc = hit if acc is None else acc + hit
            dst[pl.ds(rb * TILE, TILE), pl.ds(t * TILE, TILE)] = acc

    def build(dst, js):
        def one_strip(rb, c):
            strip(dst, rb, js)
            return c

        lax.fori_loop(0, tiles, one_strip, 0)

    def gather_sum(out, counts, table, js=None):
        def step(kb, c):
            if js is not None:
                strip(counts, 2 * kb, js)
                strip(counts, 2 * kb + 1, js)
            rows = pl.ds(kb * BIG, BIG)
            out[...] += dot_rows(counts[rows, :], table[rows, :])
            return c

        lax.fori_loop(0, nodes // BIG, step, 0)

    def in_blocks(fn, size=BIG):
        def step(nb, c):
            fn(pl.ds(nb * size, size))
            return c

        lax.fori_loop(0, nodes // size, step, 0)

    def dot(a, b):
        return jnp.dot(a, b, preferred_element_type=F32)

    def dot_rows(a, b):
        return lax.dot_general(a, b, (((0,), (0,)), ((), ())), preferred_element_type=F32)

    def dot_cols(a, b):
        return lax.dot_general(a, b, (((1,), (1,)), ((), ())), preferred_element_type=F32)

    build(t_list, lists)
    gf_ref[...] = jnp.zeros_like(gf_ref)

    pl.semaphore_wait(barrier, total - 1)

    hub_all[pl.ds(me * bnd, bnd), :] = hub_ref[...]
    each_chip(
        lambda y2, c2: remote(
            hub_ref, hub_all.at[pl.ds(me * bnd, bnd)], s_send.at[0], s_hub, (y2 * 2 + core, c2)
        ).start()
    )

    def send_row(i, count, src, dst, ssem, rsem):
        r2 = far_row(i)
        for c2 in far_cols[:count]:
            remote(src.at[r2 * cols_n + c2], dst.at[me], ssem, rsem, (r2, c2)).start()

    x_copy.wait()
    gather_sum(gf_ref, t_list, x_ref)
    send1[...] = gf_ref[...].astype(BF16).reshape(total, bnd, width)

    def send_picked(i, c):
        send_row(i, cols_n, send1, recv1, s_send.at[1], s_bnd.at[i // 2])
        return c

    lax.fori_loop(0, rows_n - 1, send_picked, 0)
    send_row(rows_n - 1, cols_n - 1, send1, recv1, s_send.at[1], s_bnd.at[rows_n // 2 - 1])
    recv1[me] = send1[me]

    gf_ref[...] = jnp.zeros_like(gf_ref)
    gather_sum(gf_ref, t_loc, x_ref, local)

    def own_part(rows):
        pre_ref[rows, :] = dot(x_ref[rows, :], ws_ref[...]) + bias_ref[...]

    in_blocks(own_part)

    drain(hub_all.at[pl.ds(0, (chips - 1) * bnd)], s_hub)
    for y2 in range(rows_n // 2):
        part = hub_all.at[pl.ds((y2 * 2 + core) * TILE, TILE)]
        remote(part, part, s_send.at[2], s_hubp, partner).start()

    build(t_rem, remotes)
    drain(hub_all.at[pl.ds(0, rows_n // 2 * TILE)], s_hubp)

    gather_sum(gf_ref, t_hub, hub_all, hubs)

    def remote_part(i):
        y2 = lax.rem(yy + 4 - far(i), 4)
        incoming = recv1[pl.ds(y2 * 2 * cols_n, 2 * cols_n)].reshape(BIG, width)
        gf_ref[...] += dot_rows(t_rem[pl.ds(pl.multiple_of(y2 * BIG, BIG), BIG), :], incoming)

    def remote_step(i, c):
        drain(recv1.at[pl.ds(0, 2 * cols_n)], s_bnd.at[i])
        remote_part(i)
        return c

    lax.fori_loop(0, rows_n // 2 - 1, remote_step, 0)
    drain(recv1.at[pl.ds(0, 2 * cols_n - 1)], s_bnd.at[rows_n // 2 - 1])
    cot_copy.wait()
    remote_part(jnp.int32(rows_n // 2 - 1))

    def dense(rows):
        mean = (gf_ref[rows, :] / float(fanout)).astype(BF16)
        mean_ref[rows, :] = mean
        pre = pre_ref[rows, :] + dot(mean, wn_ref[...])
        sig = jax.nn.sigmoid(pre)
        act_ref[rows, :] = (pre * sig).astype(BF16)
        gp = (cot_ref[rows, :].astype(F32) * sig * (1.0 + pre * (1.0 - sig))).astype(BF16)
        gp_ref[rows, :] = gp
        gm[rows, :] = (dot_cols(gp, wn_ref[...]) / float(fanout)).astype(BF16)

    in_blocks(dense, 2 * BIG)
    act_copy = pltpu.make_async_copy(act_ref, act_out, s_io.at[2])
    act_copy.start()


    def spread_and_send(i, c):
        y2 = lax.rem(yy + far(i), 4)
        out = dot(t_rem[pl.ds(pl.multiple_of(y2 * BIG, BIG), BIG), :], gm[...]).astype(BF16)
        send2[pl.ds(y2 * 2 * cols_n, 2 * cols_n)] = out.reshape(2 * cols_n, bnd, width)
        return c

    def spread_step(i, c):
        spread_and_send(i, 0)
        send_row(2 * i, cols_n, send2, recv2, s_send.at[5], s_gb)
        send_row(2 * i + 1, cols_n, send2, recv2, s_send.at[5], s_gb)
        return c

    lax.fori_loop(0, rows_n // 2 - 1, spread_step, 0)
    spread_and_send(jnp.int32(rows_n // 2 - 1), 0)
    send_row(rows_n - 2, cols_n, send2, recv2, s_send.at[5], s_gb)
    send_row(rows_n - 1, cols_n - 1, send2, recv2, s_send.at[5], s_gb)
    recv2[me] = send2[me]

    wpart[...] = jnp.zeros_like(wpart)
    bpart[...] = jnp.zeros_like(bpart)

    def weight_part(rows):
        gp = gp_ref[rows, :]
        wpart[0] += dot_rows(x_ref[rows, :], gp)
        wpart[1] += dot_rows(mean_ref[rows, :], gp)
        bpart[0:1, :] += jnp.sum(gp.astype(F32), axis=0, keepdims=True)

    in_blocks(weight_part)
    remote(wpart.at[1 - core], wpair, s_send.at[3], s_wpair.at[0], partner).start()
    remote(bpart, bpair, s_send.at[4], s_wpair.at[1], partner).start()

    def hub_part(rows):
        hub_own[rows, :] = dot(t_hub[rows, :], gm[...])

    in_blocks(hub_part, 2 * BIG)
    for y2 in range(rows_n // 2):
        pair_out[pl.ds(y2 * TILE, TILE), :] = hub_own[
            pl.ds(pl.multiple_of((y2 * 2 + 1 - core) * TILE, TILE), TILE), :
        ].astype(BF16)
    remote(pair_out, pair_in, s_send.at[8], s_gpair, partner).start()

    drain(wpair, s_wpair.at[0])
    drain(bpair, s_wpair.at[1])
    both = wpart[core] + wpair[...]
    for h in range(2):
        wsend[pl.ds(h * (chips // 2), chips // 2)] = (
            both[:, h * 128 : h * 128 + 128].astype(BF16).reshape(chips // 2, 8, 128)
        )
    brecv[chip] = bpart[0:1, :] + bpair[0:1, :]

    def send_weights(y2, c2):
        dev = (y2 * 2 + core, c2)
        remote(wsend.at[y2 * cols_n + c2], wrecv.at[chip], s_send.at[6], s_w, dev).start()
        remote(brecv.at[chip], brecv.at[chip], s_send.at[7], s_b, dev).start()

    each_chip(send_weights)
    wrecv[chip] = wsend[chip]
    drain(pair_in, s_gpair)

    def hub_join(y2, c):
        rows = pl.ds(y2 * TILE, TILE)
        mine = hub_own[pl.ds((y2 * 2 + core) * TILE, TILE), :]
        both = (mine + pair_in[rows, :].astype(F32)).astype(BF16)
        hub_send[pl.ds(y2 * cols_n, cols_n)] = both.reshape(cols_n, bnd, width)
        return c

    lax.fori_loop(0, rows_n // 2, hub_join, 0)
    each_chip(
        lambda y2, c2: remote(
            hub_send.at[y2 * cols_n + c2],
            hub_recv.at[chip],
            s_send.at[9],
            s_ghub,
            (y2 * 2 + core, c2),
        ).start()
    )
    hub_recv[chip] = hub_send[chip]

    def local_back(rows):
        gf_ref[rows, :] = dot_cols(gp_ref[rows, :], ws_ref[...]) + dot(t_loc[rows, :], gm[...])

    in_blocks(local_back, 2 * BIG)
    drain(wrecv.at[pl.ds(0, chips - 1)], s_w)
    drain(brecv.at[pl.ds(0, chips - 1)], s_b)
    wown[...] = jnp.sum(wrecv[...].astype(F32), axis=0).astype(BF16)
    each_chip(
        lambda y2, c2: remote(
            wown, wtot.at[core, chip], s_send.at[10], s_wag, (y2 * 2 + core, c2)
        ).start()
    )
    wtot[core, chip] = wown[...]
    gb_ref[...] = jnp.sum(brecv[...], axis=0)

    drain(recv2.at[pl.ds(0, total - 1)], s_gb)


    def return_part(rows):
        gf_ref[rows, :] += dot(t_list[rows, :], recv2[...].reshape(total * bnd, width))

    in_blocks(return_part, 2 * BIG)
    gf_copy = pltpu.make_async_copy(gf_ref, gf_out, s_io.at[3])
    gf_copy.start()
    drain(wrecv.at[pl.ds(0, chips - 1)], s_wag)
    remote(wtot.at[core], wtot.at[core], s_send.at[11], s_wagp, partner).start()

    drain(hub_recv.at[pl.ds(0, chips - 1)], s_ghub)
    ghub_ref[...] = jnp.sum(hub_recv[...].astype(F32), axis=0)

    drain(wtot.at[0], s_wagp)
    for h in range(2):
        part = pl.ds(h * (chips // 2), chips // 2)
        gws_ref[:, pl.ds(h * 128, 128)] = wtot[0, part].astype(F32).reshape(width, 128)
        gwn_ref[:, pl.ds(h * 128, 128)] = wtot[1, part].astype(F32).reshape(width, 128)
    drain(hub_all.at[pl.ds(0, (chips - 1) * bnd)], s_send.at[0])
    drain(recv1.at[pl.ds(0, total - 1)], s_send.at[1])
    drain(pair_in, s_send.at[2])
    drain(wpair, s_send.at[3])
    drain(bpair, s_send.at[4])
    drain(recv1.at[pl.ds(0, total - 1)], s_send.at[5])
    drain(wrecv.at[pl.ds(0, chips - 1)], s_send.at[6])
    drain(brecv.at[pl.ds(0, chips - 1)], s_send.at[7])
    drain(pair_in, s_send.at[8])
    drain(hub_recv.at[pl.ds(0, chips - 1)], s_send.at[9])
    drain(wrecv.at[pl.ds(0, chips - 1)], s_send.at[10])
    drain(wtot.at[0], s_send.at[11])
    act_copy.wait()
    gf_copy.wait()


def write_out(pieces, *refs):
    count = len(pieces)
    sources, results, held = refs[:count], refs[count : 2 * count], refs[2 * count : 3 * count]
    arrive, leave = refs[3 * count], refs[3 * count + 1]
    steps = []
    for k, parts in enumerate(pieces):
        size = sources[k].shape[0] // parts
        for p in range(parts):
            rows = pl.ds(p * size, size)
            n = len(steps)
            steps.append(
                (
                    pltpu.make_async_copy(sources[k].at[rows], held[k].at[rows], arrive.at[n]),
                    pltpu.make_async_copy(held[k].at[rows], results[k].at[rows], leave.at[n]),
                )
            )
    for inward, outward in steps:
        inward.start()
    for inward, outward in steps:
        inward.wait()
        outward.start()
    for inward, outward in steps:
        outward.wait()


def solution(mesh):
    rows_n, cols_n = mesh.shape["row"], mesh.shape["col"]

    def body(
        features,
        hub_features,
        w_self,
        w_neigh,
        out_bias,
        local_edges,
        hub_edges,
        remote_edges,
        send_rows,
        cotangent,
    ):
        nodes, width = features.shape
        hub_own = hub_features.shape[0]
        total = rows_n * cols_n
        chips = total // 2
        bnd = send_rows.shape[1] // total
        hubs = hub_own * total
        fanouts = (local_edges.shape[1], hub_edges.shape[1], remote_edges.shape[1])
        vmem = pl.BlockSpec(memory_space=pltpu.VMEM)
        hbm = pl.BlockSpec(memory_space=pl.ANY)
        dma = pltpu.SemaphoreType.DMA
        outs = pl.pallas_call(
            functools.partial(kernel, rows_n, cols_n, fanouts),
            out_shape=(
                jax.ShapeDtypeStruct((nodes, width), BF16),
                jax.ShapeDtypeStruct((nodes, width), F32),
                jax.ShapeDtypeStruct((hub_own, width), F32),
                jax.ShapeDtypeStruct((width, width), F32),
                jax.ShapeDtypeStruct((width, width), F32),
                jax.ShapeDtypeStruct((1, width), F32),
            ),
            in_specs=[hbm] * 10,
            out_specs=(hbm, hbm) + (vmem,) * 4,
            scratch_shapes=[
                pltpu.VMEM((hub_own, width), BF16),
                pltpu.VMEM((width, width), BF16),
                pltpu.VMEM((width, width), BF16),
                pltpu.VMEM((1, width), F32),
                pltpu.VMEM((fanouts[0], nodes), jnp.int32),
                pltpu.VMEM((fanouts[1], nodes), jnp.int32),
                pltpu.VMEM((fanouts[2], nodes), jnp.int32),
                pltpu.VMEM((1, send_rows.shape[1]), jnp.int32),
                pltpu.VMEM((nodes, width), BF16),
                pltpu.VMEM((nodes, width), BF16),
                pltpu.VMEM((nodes, width), BF16),
                pltpu.VMEM((nodes, width), F32),
                pltpu.VMEM((nodes, width), BF16),
                pltpu.VMEM((nodes, width), BF16),
                pltpu.VMEM((nodes, width), F32),
                pltpu.VMEM((16, nodes), F32),
                pltpu.VMEM((nodes, nodes), BF16),
                pltpu.VMEM((hubs, nodes), BF16),
                pltpu.VMEM((total * bnd, nodes), BF16),
                pltpu.VMEM((nodes, total * bnd), BF16),
                pltpu.VMEM((total, bnd, width), BF16),
                pltpu.VMEM((total, bnd, width), BF16),
                pltpu.VMEM((hubs, width), BF16),
                pltpu.VMEM((total, bnd, width), BF16),
                pltpu.VMEM((total, bnd, width), BF16),
                pltpu.VMEM((nodes, width), BF16),
                pltpu.VMEM((hubs // 2, width), BF16),
                pltpu.VMEM((hubs // 2, width), BF16),
                pltpu.VMEM((hubs, width), F32),
                pltpu.VMEM((chips, hub_own, width), BF16),
                pltpu.VMEM((chips, hub_own, width), BF16),
                pltpu.VMEM((2, width, width), F32),
                pltpu.VMEM((width, width), F32),
                pltpu.VMEM((chips, 8, 128), BF16),
                pltpu.VMEM((chips, 8, 128), BF16),
                pltpu.VMEM((8, 128), BF16),
                pltpu.VMEM((2, chips, 8, 128), BF16),
                pltpu.VMEM((8, width), F32),
                pltpu.VMEM((8, width), F32),
                pltpu.VMEM((chips, 1, width), F32),
                dma((12,)),
                dma,
                dma,
                dma((rows_n // 2,)),
                dma((2,)),
                dma,
                dma,
                dma,
                dma,
                dma,
                dma,
                dma,
                dma((12,)),
            ],
            compiler_params=pltpu.CompilerParams(
                collective_id=0, has_side_effects=True, vmem_limit_bytes=60 << 20
            ),
        )(
            features,
            hub_features,
            w_self,
            w_neigh,
            out_bias.reshape(1, width),
            local_edges.T,
            hub_edges.T,
            remote_edges.T,
            send_rows,
            cotangent,
        )
        pieces = (2, 4, 1, 1, 1, 1)
        outs = pl.pallas_call(
            functools.partial(write_out, pieces),
            out_shape=tuple(jax.ShapeDtypeStruct(o.shape, o.dtype) for o in outs),
            in_specs=[hbm] * len(outs),
            out_specs=(hbm,) * len(outs),
            scratch_shapes=[pltpu.VMEM(o.shape, o.dtype) for o in outs]
            + [dma((sum(pieces),)), dma((sum(pieces),))],
        )(*outs)
        activated, grad_features, grad_hubs, grad_w_self, grad_w_neigh, grad_bias = outs
        return activated, grad_features, grad_hubs, grad_w_self, grad_w_neigh, grad_bias.reshape(width)

    by_node = P(("row", "col"), None)
    return jax.shard_map(
        body,
        mesh=mesh,
        in_specs=(by_node, by_node, P(), P(), P(), by_node, by_node, by_node, by_node, by_node),
        out_specs=(by_node, by_node, by_node, P(), P(), P()),
        check_vma=False,
    )
```
